32 devices in a mesh: date: 2 (over y), row: 16 (over z, x, core).
Axes of the slice: x: 2, y: 2, z: 4, core: 2. Of those that a mesh axis runs over, the one named last changes fastest.
Arguments:
- slc: float32 [2, 128, 128, 256], P(None, 'date', 'row'), may hold values from -40 to 40, as said below
- network: int32 [128, 8], replicated, may hold values 0 or 1
Outputs:
- linked: float32 [2, 128, 128, 256], P(None, None, 'row', 'date')
The draws below stay inside these ranges and needn't reach their ends.
Inputs may be any that keep to these rules, and one draw needn't show every extreme that they name: slc holds real and imaginary parts of complex samples.
All inputs are finite; a program needn't handle non-finite values.
Results may differ from the reference program's by a relative error of at most 0.0003.
Values sent between devices are 32-bit elements; how exact they have to be, the bound alone decides.
A program may use at most 192 MiB of HBM per device.

```python
import math
import jax
import jax.numpy as jnp
from jax import lax

DATES = 128
BAND = 8
LOOK = 5
ITERS = 5
ROW_DEV = 8
ROWS = 128
COLS = 256
N_ROW = 16


def draw_slc(key, part):
    keys = jax.random.split(key, 4)
    shape = (2, DATES, ROWS, COLS)
    noise = jax.random.truncated_normal(keys[0], -6.0, 6.0, shape, jnp.float32)
    amplitude = jnp.exp(jax.random.uniform(keys[1], (DATES, ROWS, COLS), jnp.float32, math.log(0.3), math.log(3.0)))
    common = 0.5
    shared = jax.random.truncated_normal(keys[2], -6.0, 6.0, (ROWS, COLS), jnp.float32)
    phases = jax.random.uniform(keys[3], (DATES,), jnp.float32, -math.pi, math.pi)
    part_re = amplitude * (noise[0] + common * shared[None] * jnp.cos(phases)[:, None, None])
    part_im = amplitude * (noise[1] + common * shared[None] * jnp.sin(phases)[:, None, None])
    return jnp.stack([part_re, part_im]).astype(jnp.float32)


def set_ends(drawn, own_key, smallest, largest):
    index_at = [jax.random.randint(jax.random.fold_in(own_key, axis), (), 0, length) for axis, length in enumerate(drawn.shape)]
    longest = drawn.shape.index(max(drawn.shape))
    next_to = index_at[:longest] + [(index_at[longest] + 1) % drawn.shape[longest]] + index_at[longest + 1:]
    return drawn.at[tuple(index_at)].set(smallest).at[tuple(next_to)].set(largest)


def setup_inputs(seed: int = 0) -> dict:
    seeds = jax.random.split(jax.random.key(seed), 3)
    slc = draw_slc(jax.random.fold_in(seeds[2], 71), 0)
    network = set_ends((jax.random.randint(seeds[1], (DATES, BAND), 0, 4) < 3).astype(jnp.int32), jax.random.fold_in(seeds[1], 1), 0, 1)
    return {"slc": slc, "network": network}


def band_table(count_out):
    count_in = count_out + 2 * LOOK
    outer = jnp.arange(count_out, dtype=jnp.int32)[:, None]
    inner = jnp.arange(count_in, dtype=jnp.int32)[None, :]
    reach = inner - outer
    return ((reach >= 0) & (reach <= 2 * LOOK)).astype(jnp.float32)

def box_sum(samples):
    rows_out = samples.shape[-2] - 2 * LOOK
    cols_out = samples.shape[-1] - 2 * LOOK
    row_table = band_table(rows_out)
    col_table = band_table(cols_out)
    total = jnp.einsum('...rc,kr->...kc', samples, row_table, precision=lax.Precision.HIGHEST)
    return jnp.einsum('...kc,mc->...km', total, col_table, precision=lax.Precision.HIGHEST)

def coherence(extended, network):
    num_dates = extended.shape[1]
    squares = extended[0] * extended[0] + extended[1] * extended[1]
    inverse_root = lax.rsqrt(box_sum(squares) + 1e-06)
    layers = []
    for offset in range(1, network.shape[1] + 1):
        earlier = extended[:, :num_dates - offset]
        later = extended[:, offset:]
        prod_re = earlier[0] * later[0] + earlier[1] * later[1]
        prod_im = earlier[1] * later[0] - earlier[0] * later[1]
        sums = box_sum(jnp.stack([prod_re, prod_im]))
        weight = network[:num_dates - offset, offset - 1].astype(jnp.float32)[:, None, None]
        weight = weight * inverse_root[:num_dates - offset] * inverse_root[offset:]
        layer = sums * weight[None]
        layers.append(jnp.pad(layer, ((0, 0), (0, offset), (0, 0), (0, 0))))
    return jnp.stack(layers)

def apply_matrix(coherent, vector):
    num_dates = vector.shape[1]
    image_re = vector[0]
    image_im = vector[1]
    for offset in range(1, coherent.shape[0] + 1):
        coh_re = coherent[offset - 1, 0]
        coh_im = coherent[offset - 1, 1]
        ahead = jnp.pad(vector[:, offset:], ((0, 0), (0, offset), (0, 0), (0, 0)))
        image_re = image_re + coh_re * ahead[0] - coh_im * ahead[1]
        image_im = image_im + coh_re * ahead[1] + coh_im * ahead[0]
        back_re = coh_re * vector[0] + coh_im * vector[1]
        back_im = coh_re * vector[1] - coh_im * vector[0]
        image_re = image_re + jnp.pad(back_re[:num_dates - offset], ((offset, 0), (0, 0), (0, 0)))
        image_im = image_im + jnp.pad(back_im[:num_dates - offset], ((offset, 0), (0, 0), (0, 0)))
    image = jnp.stack([image_re, image_im])
    meansq = lax.optimization_barrier(jnp.mean(image[0] * image[0] + image[1] * image[1], axis=0))
    return image * lax.rsqrt(meansq + 1e-06)[None, None]

def power_iterate(coherent):
    start = jnp.stack([jnp.ones_like(coherent[0, 0]), jnp.zeros_like(coherent[0, 0])])

    def iterate_once(index, vector):
        return apply_matrix(coherent, vector)
    return lax.fori_loop(0, ITERS, iterate_once, start)

def reference(slc, network):
    padded = jnp.pad(slc, ((0, 0), (0, 0), (LOOK, LOOK), (LOOK, LOOK)))

    def one_strip(strip):
        first = (strip * ROW_DEV).astype(jnp.int32)
        extended = lax.dynamic_slice_in_dim(padded, first, ROW_DEV + 2 * LOOK, 2)
        return power_iterate(coherence(extended, network))
    strips = lax.map(one_strip, jnp.arange(N_ROW, dtype=jnp.int32))
    strips = jnp.transpose(strips, (1, 2, 0, 3, 4))
    return strips.reshape(2, DATES, ROWS, COLS)
```

```python
import functools

import jax
import jax.numpy as jnp
from jax import lax
from jax.experimental import pallas as pl
from jax.experimental.pallas import tpu as pltpu
from jax.sharding import PartitionSpec as P

LOOK = 5
ITERS = 5
SUB = 8
CHUNK = 16
EPS = 1e-06
MESH = pl.DeviceIdType.MESH


def row_sums(cells):
    span = 2 * LOOK + 1
    count = len(cells) - span + 1
    head = functools.reduce(jnp.add, cells[count - 1 : span])
    heads = [head]
    for k in range(count - 2, -1, -1):
        heads.append(heads[-1] + cells[k])
    heads = heads[::-1]
    sums = [heads[0]]
    tail = None
    for k in range(1, count):
        cell = cells[span + k - 1]
        tail = cell if tail is None else tail + cell
        sums.append(heads[k] + tail)
    return sums


def halves(sums):
    stacked = jnp.concatenate(sums, axis=0)
    high = stacked.astype(jnp.bfloat16)
    low = (stacked - high.astype(jnp.float32)).astype(jnp.bfloat16)
    return jnp.concatenate([high, low], axis=1)


def products(load, offset, depth):
    if offset == 0:
        squares = []
        for r in range(depth):
            re, im = load(0, r, 0), load(1, r, 0)
            squares.append(re * re + im * im)
        return row_sums(squares)
    part_re, part_im = [], []
    for r in range(depth):
        a_re, a_im = load(0, r, offset), load(1, r, offset)
        b_re, b_im = load(0, r, 0), load(1, r, 0)
        part_re.append(a_re * b_re + a_im * b_im)
        part_im.append(a_im * b_re - a_re * b_im)
    return row_sums(part_re) + row_sums(part_im)


def main_kernel(
    nd, nr, x_hbm, net_ref, vec, tot,
    x_ref, packed, packed_rim, main, rim, rim_maps, table, root, used_at, gam, acc, load_sem,
    give_send, give_recv, up_send, up_recv, down_send, down_recv,
):
    _, local, rows, _ = x_ref.shape
    width = main.shape[3]
    band, dates = net_ref.shape
    groups = local // SUB
    slot = width // groups
    tiles = dates // SUB
    tall = rows + 2 * LOOK
    parts = give_send.shape[1] - 1
    piece = local // parts
    span = piece // SUB
    me = lax.axis_index("date")
    row = lax.axis_index("row")
    has_up = row > 0
    has_down = row < nr - 1
    up = jnp.maximum(row - 1, 0)
    down = jnp.minimum(row + 1, nr - 1)

    def mirrored(device):
        return 2 * device >= nd

    def place(source, device):
        return jnp.where(mirrored(device), nd - 1 - source, source)

    def source_of(k):
        return lax.rem(me + nd - k, nd)

    barrier = pltpu.get_barrier_semaphore()
    for k in range(1, nd):
        pl.semaphore_signal(barrier, 1, device_id=(lax.rem(me + k, nd), row), device_id_type=MESH)

    @pl.when(has_up)
    def _():
        pl.semaphore_signal(barrier, 1, device_id=(me, up), device_id_type=MESH)

    @pl.when(has_down)
    def _():
        pl.semaphore_signal(barrier, 1, device_id=(me, down), device_id_type=MESH)

    fetch = pltpu.make_async_copy(x_hbm, x_ref, load_sem)
    fetch.start()

    def give(k, n):
        there = lax.rem(me + k, nd)
        at = place(me, there)
        if n == 0:
            src = packed_rim.at[k - 1]
            dst = rim.at[at, :, pl.ds(LOOK, rows), pl.ds(SUB, SUB)]
        else:
            src = packed.at[k - 1, :, :, pl.ds((n - 1) * piece, piece)]
            begin = pl.multiple_of(SUB + at * local + (n - 1) * piece, SUB)
            dst = main.at[:, pl.ds(LOOK, rows), pl.ds(begin, piece)]
        return pltpu.make_async_remote_copy(
            src_ref=src,
            dst_ref=dst,
            send_sem=give_send.at[k, n],
            recv_sem=give_recv.at[k, n],
            device_id=(there, row),
            device_id_type=MESH,
        )

    def halo(slab, n, to_up, is_rim):
        first = LOOK if to_up else rows
        land = LOOK + rows if to_up else 0
        if is_rim:
            src = rim.at[slab, :, pl.ds(first, LOOK), pl.ds(SUB, SUB)]
            dst = rim.at[slab, :, pl.ds(land, LOOK), pl.ds(SUB, SUB)]
        else:
            near = pl.ds(pl.multiple_of(SUB + slab * local + (n - 1) * piece, SUB), piece)
            src = main.at[:, pl.ds(first, LOOK), near]
            dst = main.at[:, pl.ds(land, LOOK), near]
        return pltpu.make_async_remote_copy(
            src_ref=src,
            dst_ref=dst,
            send_sem=(up_send if to_up else down_send).at[slab, n],
            recv_sem=(up_recv if to_up else down_recv).at[slab, n],
            device_id=(me, up if to_up else down),
            device_id_type=MESH,
        )

    def start_halos(slab, n, is_rim):
        @pl.when(has_up)
        def _():
            halo(slab, n, True, is_rim).start()

        @pl.when(has_down)
        def _():
            halo(slab, n, False, is_rim).start()

    def await_halos(slab, n, is_rim):
        @pl.when(has_up)
        def _():
            halo(slab, n, False, is_rim).wait_recv()

        @pl.when(has_down)
        def _():
            halo(slab, n, True, is_rim).wait_recv()

    def forward(k, n):
        give(k, n).wait_recv()
        start_halos(place(source_of(k), me), n, n == 0)

    zero = jnp.zeros((rows, width), jnp.float32)
    blank = jnp.zeros((SUB, width), jnp.float32)

    @pl.when(jnp.logical_not(has_up))
    def _():
        for comp in range(2):
            for r in range(LOOK):
                main[comp, r] = jnp.zeros((SUB + dates, width), jnp.float32)
                for s in range(nd):
                    rim[s, comp, r, pl.ds(SUB, SUB)] = blank

    @pl.when(jnp.logical_not(has_down))
    def _():
        for comp in range(2):
            for r in range(LOOK + rows, tall):
                main[comp, r] = jnp.zeros((SUB + dates, width), jnp.float32)
                for s in range(nd):
                    rim[s, comp, r, pl.ds(SUB, SUB)] = blank

    for comp in range(2):
        for r in range(tall):
            main[comp, r, pl.ds(0, SUB)] = blank

    fetch.wait()
    lane = lax.broadcasted_iota(jnp.int32, (rows, width), 1)

    def turned(tiles_of_dates):
        return jnp.transpose(jnp.stack(tiles_of_dates), (1, 0, 2))

    def pack(device, put):
        turn = mirrored(device)
        column = pl.ds(pl.multiple_of(device * width, width), width)

        def group(g, carry):
            for comp in range(2):
                cells = []
                for j in range(SUB):
                    d = g * SUB + j
                    cells.append(x_ref[comp, jnp.where(turn, local - 1 - d, d), :, column])
                put(comp, pl.ds(pl.multiple_of(g * SUB, SUB), SUB), turned(cells))
            return carry

        lax.fori_loop(0, groups, group, 0)

    def pack_rim(device, put):
        turn = mirrored(device)
        if nd == 2:
            sides = [(1 - device, 0, 2 * LOOK)]
        else:
            sides = [(jnp.maximum(device - 1, 0), 0, LOOK), (jnp.minimum(device + 1, nd - 1), LOOK, 2 * LOOK)]
        for comp in range(2):
            cells = []
            for j in range(SUB):
                cell = zero
                for g in range(groups):
                    d = g * SUB + j
                    d = jnp.where(turn, local - 1 - d, d)
                    first = slot * g
                    for block, low, high in sides:
                        column = pl.ds(pl.multiple_of(block * width, width), width)
                        moved = pltpu.roll(x_ref[comp, d, :, column], (first + LOOK) % width, 1)
                        cell = jnp.where((lane >= first + low) & (lane < first + high), moved, cell)
                cells.append(cell)
            put(comp, turned(cells))

    own = place(me, me)

    def put_own(comp, near, tile):
        begin = pl.multiple_of(SUB + own * local + near.start, SUB)
        main[comp, pl.ds(LOOK, rows), pl.ds(begin, SUB)] = tile

    def put_own_rim(comp, tile):
        rim[own, comp, pl.ds(LOOK, rows), pl.ds(SUB, SUB)] = tile

    pack_rim(me, put_own_rim)
    pack(me, put_own)
    for k in range(1, nd):
        there = lax.rem(me + k, nd)

        def put_rim(comp, tile, k=k):
            packed_rim[k - 1, comp] = tile

        def put_main(comp, near, tile, k=k):
            packed[k - 1, comp, :, near] = tile

        pack_rim(there, put_rim)
        pack(there, put_main)

    pl.semaphore_wait(barrier, nd - 1 + has_up.astype(jnp.int32) + has_down.astype(jnp.int32))
    for n in range(parts + 1):
        for k in range(1, nd):
            give(k, n).start()
        start_halos(own, n, n == 0)

    inner = lax.broadcasted_iota(jnp.int32, (width, width), 0)
    outer = lax.broadcasted_iota(jnp.int32, (width, width), 1)
    box = (jnp.abs(inner - outer) <= LOOK).astype(jnp.float32).astype(jnp.bfloat16)
    for g in range(groups):
        cell = inner - slot * g
        left = (cell >= 0) & (cell < LOOK) & (outer <= cell) & (me > 0)
        right = (cell >= LOOK) & (cell < 2 * LOOK) & (outer >= width + cell - 2 * LOOK) & (me < nd - 1)
        edge = (left | right).astype(jnp.float32).astype(jnp.bfloat16)
        for begin, part in ((0, box), (1, box), (2, edge), (3, edge)):
            table[g, pl.ds(begin * width, width)] = part

    turn = mirrored(me)
    inner = lax.broadcasted_iota(jnp.int32, (dates, dates), 0)
    outer = lax.broadcasted_iota(jnp.int32, (dates, dates), 1)
    order = (inner == jnp.where(turn, dates - 1 - outer, outer)).astype(jnp.float32).astype(jnp.bfloat16)
    mask = jnp.transpose(net_ref[...].astype(jnp.float32), (1, 0)).astype(jnp.bfloat16)
    used_at[pl.ds(0, SUB)] = jnp.zeros((SUB, band), jnp.float32)
    used_at[pl.ds(SUB, dates)] = jnp.dot(order, mask, preferred_element_type=jnp.float32)

    for k in range(rows):
        root[k, pl.ds(0, SUB)] = blank
    for comp in range(2):
        for step in range(ITERS):
            for d in range(band):
                vec[step, comp, dates + d] = zero
    for step in range(ITERS):
        tot[step] = zero
        for c in range(3):
            for d in range(band):
                acc[step, c, d] = zero
    for c in range(3):
        for o in range(band):
            gam[c, o, pl.ds(dates * rows, band * rows)] = jnp.zeros((band * rows, width), jnp.float32)

    if nd != 2:
        for n in range(parts + 1):
            for k in range(1, nd):
                forward(k, n)

    lane = lax.broadcasted_iota(jnp.int32, (SUB, width), 1)

    def rim_sums(slab):
        before = jnp.maximum(slab - 1, 0)
        for comp in range(2):
            for r in range(tall):
                earlier = pltpu.roll(rim[slab, comp, r, pl.ds(SUB, SUB)], slot % width, 1)
                last = pltpu.roll(rim[before, comp, r, pl.ds(SUB, SUB)], (width - slot * (groups - 1)) % width, 1)
                last = jnp.where(slab > 0, last, 0.0)
                rim[slab, comp, r, pl.ds(0, SUB)] = jnp.where(lane < slot, last, earlier)

        def load(comp, r, offset):
            return rim[slab, comp, r, pl.ds(SUB - offset, SUB)]

        begin = 0
        for offset in range(band + 1):
            maps = halves(products(load, offset, tall))
            rim_maps[pl.ds(begin, maps.shape[0])] = maps
            begin += maps.shape[0]

    def tile_sums(t):
        g = lax.rem(t, groups)
        base = t * SUB
        here = pl.ds(pl.multiple_of(base + SUB, SUB), SUB)

        def load(comp, r, offset):
            return main[comp, r, here if offset == 0 else pl.ds(base + SUB - offset, SUB)]

        begin = 0
        for offset in range(band + 1):
            maps = halves(products(load, offset, tall))
            count = maps.shape[0]
            maps = jnp.concatenate([maps, rim_maps[pl.ds(begin, count)]], axis=1)
            begin += count
            sums = jnp.dot(maps, table[g], preferred_element_type=jnp.float32)
            if offset == 0:
                for k in range(rows):
                    root[k, here] = lax.rsqrt(sums[k * SUB : (k + 1) * SUB] + EPS)
                continue
            used = used_at[pl.ds(base + SUB - jnp.where(turn, 0, offset), SUB), :]
            used = used[:, offset - 1 : offset]
            for k in range(rows):
                weight = root[k, here] * root[k, pl.ds(base + SUB - offset, SUB)]
                weight = weight * used
                at = pl.ds((band + base - offset) * rows + k, SUB, stride=rows)
                c_re = sums[k * SUB : (k + 1) * SUB] * weight
                c_im = sums[(rows + k) * SUB : (rows + k + 1) * SUB] * weight
                gam[0, offset - 1, at] = c_re
                gam[1, offset - 1, at] = c_re + c_im
                gam[2, offset - 1, at] = c_im - c_re

    def at_date(d):
        return pl.ds(pl.multiple_of((band + d) * rows, rows), rows)

    def first(j):
        back_re = [acc[0, 0, i] for i in range(band)]
        back_sum = [acc[0, 1, i] for i in range(band)]
        total = tot[0]
        for i in range(SUB):
            d = j * SUB + i
            y_re = back_re[i] + 1.0
            y_im = back_re[i] - back_sum[i]
            ahead_re = ahead_sum = None
            for o in range(1, band + 1):
                c_re = gam[0, o - 1, at_date(d)]
                c_sum = gam[1, o - 1, at_date(d)]
                ahead_re = c_re if ahead_re is None else ahead_re + c_re
                ahead_sum = c_sum if ahead_sum is None else ahead_sum + c_sum
                if o == band:
                    back_re.append(c_re)
                    back_sum.append(c_sum)
                else:
                    back_re[i + o] = back_re[i + o] + c_re
                    back_sum[i + o] = back_sum[i + o] + c_sum
            y_re = y_re + ahead_re
            y_im = y_im + (ahead_sum - ahead_re)
            vec[0, 0, d] = y_re
            vec[0, 1, d] = y_im
            total = total + (y_re * y_re + y_im * y_im)
        for i in range(band):
            acc[0, 0, i] = back_re[SUB + i]
            acc[0, 1, i] = back_sum[SUB + i]
        tot[0] = total

    def later(step, j):
        acc_a, acc_b, acc_c = [[acc[step, c, i] for i in range(band)] for c in range(3)]
        base = j * SUB
        v_re = [vec[step - 1, 0, base + i] for i in range(band)]
        v_im = [vec[step - 1, 1, base + i] for i in range(band)]
        v_sum = [a + b for a, b in zip(v_re, v_im)]
        total = tot[step]
        for i in range(SUB):
            d = base + i
            v_re.append(vec[step - 1, 0, d + band])
            v_im.append(vec[step - 1, 1, d + band])
            v_sum.append(v_re[-1] + v_im[-1])
            y_a, y_b, y_c = acc_a[i], -acc_b[i], -acc_c[i]
            for o in range(1, band + 1):
                c_re = gam[0, o - 1, at_date(d)]
                c_sum = gam[1, o - 1, at_date(d)]
                c_dif = gam[2, o - 1, at_date(d)]
                y_a = y_a + c_re * v_sum[i + o]
                y_b = y_b + c_dif * v_re[i + o]
                y_c = y_c + c_sum * v_im[i + o]
                back_a = c_re * v_sum[i]
                back_b = c_sum * v_re[i]
                back_c = c_dif * v_im[i]
                if o == band:
                    acc_a.append(back_a)
                    acc_b.append(back_b)
                    acc_c.append(back_c)
                else:
                    acc_a[i + o] = acc_a[i + o] + back_a
                    acc_b[i + o] = acc_b[i + o] + back_b
                    acc_c[i + o] = acc_c[i + o] + back_c
            y_re = v_re[i] + (y_a - y_c)
            y_im = v_im[i] + (y_a + y_b)
            vec[step, 0, d] = y_re
            vec[step, 1, d] = y_im
            total = total + (y_re * y_re + y_im * y_im)
        for i in range(band):
            acc[step, 0, i] = acc_a[SUB + i]
            acc[step, 1, i] = acc_b[SUB + i]
            acc[step, 2, i] = acc_c[SUB + i]
        tot[step] = total

    def advance(t, carry):
        if nd == 2:
            for n in range(parts + 1):

                @pl.when(t == (groups * 5 * n) // (4 * parts))
                def _(n=n):
                    forward(1, n)

        @pl.when(t < tiles)
        def _():
            slab = lax.div(t, groups)
            g = lax.rem(t, groups)

            @pl.when(lax.rem(g, span) == 0)
            def _():
                await_halos(slab, 1 + lax.div(g, span), False)

            @pl.when(g == 0)
            def _():
                await_halos(slab, 0, True)
                rim_sums(slab)

            tile_sums(t)

        @pl.when((t >= 1) & (t <= tiles))
        def _():
            first(t - 1)

        def level(step, carry):
            later(step, t - 1 - step)
            return carry

        lax.fori_loop(jnp.maximum(1, t - tiles), jnp.minimum(t, ITERS), level, 0)
        return carry

    lax.fori_loop(0, tiles + ITERS, advance, 0)

    for n in range(parts + 1):
        for k in range(1, nd):
            give(k, n).wait_send()
        for s in range(nd):

            @pl.when(has_up)
            def _():
                halo(s, n, True, n == 0).wait_send()

            @pl.when(has_down)
            def _():
                halo(s, n, False, n == 0).wait_send()


def scale_kernel(nd, vec, tot, out_ref):
    dates = out_ref.shape[1]
    scale = None
    for step in range(ITERS):
        mean = tot[step] / dates
        if scale is None:
            scale = lax.rsqrt(mean + EPS)
        else:
            scale = scale * lax.rsqrt(scale * scale * mean + EPS)
    turn = 2 * lax.axis_index("date") >= nd

    def block(b, carry):
        for j in range(SUB):
            d = b * SUB + j
            at = jnp.where(turn, dates - 1 - d, d)
            for comp in range(2):
                out_ref[comp, at] = vec[ITERS - 1, comp, d] * scale
        return carry

    lax.fori_loop(0, dates // SUB, block, 0)


def on_device(nd, nr, slc, network):
    _, local, rows, cols = slc.shape
    width = cols // nd
    dates, band = network.shape
    tall = rows + 2 * LOOK
    maps = (2 * band + 1) * rows * SUB
    parts = local // CHUNK if local % CHUNK == 0 else 1
    whole = pl.BlockSpec(memory_space=pltpu.VMEM)
    away = pl.BlockSpec(memory_space=pl.ANY)
    f32 = jnp.float32
    give_sems = pltpu.SemaphoreType.DMA((nd, parts + 1))
    vec, tot = pl.pallas_call(
        functools.partial(main_kernel, nd, nr),
        out_shape=[
            pltpu.VMEM((ITERS, 2, dates + band, rows, width), f32),
            pltpu.VMEM((ITERS, rows, width), f32),
        ],
        in_specs=[away, whole],
        out_specs=[whole, whole],
        scratch_shapes=[
            pltpu.VMEM((2, local, rows, cols), f32),
            pltpu.VMEM((nd - 1, 2, rows, local, width), f32),
            pltpu.VMEM((nd - 1, 2, rows, SUB, width), f32),
            pltpu.VMEM((2, tall, SUB + dates, width), f32),
            pltpu.VMEM((nd, 2, tall, 2 * SUB, width), f32),
            pltpu.VMEM((maps, 2 * width), jnp.bfloat16),
            pltpu.VMEM((local // SUB, 4 * width, width), jnp.bfloat16),
            pltpu.VMEM((rows, SUB + dates, width), f32),
            pltpu.VMEM((SUB + dates, band), f32),
            pltpu.VMEM((3, band, (band + dates) * rows, width), f32),
            pltpu.VMEM((ITERS, 3, band, rows, width), f32),
            pltpu.SemaphoreType.DMA(()),
        ]
        + [give_sems] * 6,
        compiler_params=pltpu.CompilerParams(
            collective_id=0, has_side_effects=True, vmem_limit_bytes=48 * 1024 * 1024
        ),
        name="link",
    )(slc, network.T)
    return pl.pallas_call(
        functools.partial(scale_kernel, nd),
        out_shape=jax.ShapeDtypeStruct((2, dates, rows, width), f32),
        in_specs=[whole, whole],
        out_specs=whole,
        name="scale",
    )(vec, tot)


def solution(mesh):
    return jax.shard_map(
        functools.partial(on_device, mesh.shape["date"], mesh.shape["row"]),
        mesh=mesh,
        in_specs=(P(None, "date", "row", None), P()),
        out_specs=P(None, None, "row", "date"),
        check_vma=False,
    )
```

```python
import functools

import jax
import jax.numpy as jnp
from jax import lax
from jax.experimental import pallas as pl
from jax.experimental.pallas import tpu as pltpu
from jax.sharding import PartitionSpec as P

LOOK = 5
ITERS = 5
SUB = 8
CHUNK = 16
EPS = 1e-06
MESH = pl.DeviceIdType.MESH


def row_sums(cells):
    span = 2 * LOOK + 1
    count = len(cells) - span + 1
    head = functools.reduce(jnp.add, cells[count - 1 : span])
    heads = [head]
    for k in range(count - 2, -1, -1):
        heads.append(heads[-1] + cells[k])
    heads = heads[::-1]
    sums = [heads[0]]
    tail = None
    for k in range(1, count):
        cell = cells[span + k - 1]
        tail = cell if tail is None else tail + cell
        sums.append(heads[k] + tail)
    return sums


def halves(sums):
    stacked = jnp.concatenate(sums, axis=0)
    high = stacked.astype(jnp.bfloat16)
    low = (stacked - high.astype(jnp.float32)).astype(jnp.bfloat16)
    return jnp.concatenate([high, low], axis=1)


def products(load, offset, depth):
    if offset == 0:
        squares = []
        for r in range(depth):
            re, im = load(0, r, 0), load(1, r, 0)
            squares.append(re * re + im * im)
        return row_sums(squares)
    part_re, part_im = [], []
    for r in range(depth):
        a_re, a_im = load(0, r, offset), load(1, r, offset)
        b_re, b_im = load(0, r, 0), load(1, r, 0)
        part_re.append(a_re * b_re + a_im * b_im)
        part_im.append(a_im * b_re - a_re * b_im)
    return row_sums(part_re) + row_sums(part_im)


def main_kernel(
    nd, nr, x_hbm, net_ref, vec, tot,
    x_ref, packed, packed_rim, main, rim, rim_maps, table, root, used_at, gam, acc, load_sem,
    give_send, give_recv, up_send, up_recv, down_send, down_recv,
):
    _, local, rows, _ = x_ref.shape
    width = main.shape[3]
    band, dates = net_ref.shape
    groups = local // SUB
    slot = width // groups
    tiles = dates // SUB
    tall = rows + 2 * LOOK
    parts = give_send.shape[1] - 1
    piece = local // parts
    span = piece // SUB
    me = lax.axis_index("date")
    row = lax.axis_index("row")
    has_up = row > 0
    has_down = row < nr - 1
    up = jnp.maximum(row - 1, 0)
    down = jnp.minimum(row + 1, nr - 1)

    def mirrored(device):
        return 2 * device >= nd

    def place(source, device):
        return jnp.where(mirrored(device), nd - 1 - source, source)

    def source_of(k):
        return lax.rem(me + nd - k, nd)

    barrier = pltpu.get_barrier_semaphore()
    for k in range(1, nd):
        pl.semaphore_signal(barrier, 1, device_id=(lax.rem(me + k, nd), row), device_id_type=MESH)

    @pl.when(has_up)
    def _():
        pl.semaphore_signal(barrier, 1, device_id=(me, up), device_id_type=MESH)

    @pl.when(has_down)
    def _():
        pl.semaphore_signal(barrier, 1, device_id=(me, down), device_id_type=MESH)

    fetch = pltpu.make_async_copy(x_hbm, x_ref, load_sem)
    fetch.start()

    def give(k, n):
        there = lax.rem(me + k, nd)
        at = place(me, there)
        if n == 0:
            src = packed_rim.at[k - 1]
            dst = rim.at[at, :, pl.ds(LOOK, rows), pl.ds(SUB, SUB)]
        else:
            src = packed.at[k - 1, :, :, pl.ds((n - 1) * piece, piece)]
            begin = pl.multiple_of(SUB + at * local + (n - 1) * piece, SUB)
            dst = main.at[:, pl.ds(LOOK, rows), pl.ds(begin, piece)]
        return pltpu.make_async_remote_copy(
            src_ref=src,
            dst_ref=dst,
            send_sem=give_send.at[k, n],
            recv_sem=give_recv.at[k, n],
            device_id=(there, row),
            device_id_type=MESH,
        )

    def halo(slab, n, to_up, is_rim):
        first = LOOK if to_up else rows
        land = LOOK + rows if to_up else 0
        if is_rim:
            src = rim.at[slab, :, pl.ds(first, LOOK), pl.ds(SUB, SUB)]
            dst = rim.at[slab, :, pl.ds(land, LOOK), pl.ds(SUB, SUB)]
        else:
            near = pl.ds(pl.multiple_of(SUB + slab * local + (n - 1) * piece, SUB), piece)
            src = main.at[:, pl.ds(first, LOOK), near]
            dst = main.at[:, pl.ds(land, LOOK), near]
        return pltpu.make_async_remote_copy(
            src_ref=src,
            dst_ref=dst,
            send_sem=(up_send if to_up else down_send).at[slab, n],
            recv_sem=(up_recv if to_up else down_recv).at[slab, n],
            device_id=(me, up if to_up else down),
            device_id_type=MESH,
        )

    def start_halos(slab, n, is_rim):
        @pl.when(has_up)
        def _():
            halo(slab, n, True, is_rim).start()

        @pl.when(has_down)
        def _():
            halo(slab, n, False, is_rim).start()

    def await_halos(slab, n, is_rim):
        @pl.when(has_up)
        def _():
            halo(slab, n, False, is_rim).wait_recv()

        @pl.when(has_down)
        def _():
            halo(slab, n, True, is_rim).wait_recv()

    def forward(k, n):
        give(k, n).wait_recv()
        start_halos(place(source_of(k), me), n, n == 0)

    zero = jnp.zeros((rows, width), jnp.float32)
    blank = jnp.zeros((SUB, width), jnp.float32)

    @pl.when(jnp.logical_not(has_up))
    def _():
        for comp in range(2):
            for r in range(LOOK):
                main[comp, r] = jnp.zeros((SUB + dates, width), jnp.float32)
                for s in range(nd):
                    rim[s, comp, r, pl.ds(SUB, SUB)] = blank

    @pl.when(jnp.logical_not(has_down))
    def _():
        for comp in range(2):
            for r in range(LOOK + rows, tall):
                main[comp, r] = jnp.zeros((SUB + dates, width), jnp.float32)
                for s in range(nd):
                    rim[s, comp, r, pl.ds(SUB, SUB)] = blank

    for comp in range(2):
        for r in range(tall):
            main[comp, r, pl.ds(0, SUB)] = blank

    fetch.wait()
    lane = lax.broadcasted_iota(jnp.int32, (rows, width), 1)

    def turned(tiles_of_dates):
        return jnp.transpose(jnp.stack(tiles_of_dates), (1, 0, 2))

    def pack(device, put):
        turn = mirrored(device)
        column = pl.ds(pl.multiple_of(device * width, width), width)

        def group(g, carry):
            for comp in range(2):
                cells = []
                for j in range(SUB):
                    d = g * SUB + j
                    cells.append(x_ref[comp, jnp.where(turn, local - 1 - d, d), :, column])
                put(comp, pl.ds(pl.multiple_of(g * SUB, SUB), SUB), turned(cells))
            return carry

        lax.fori_loop(0, groups, group, 0)

    def pack_rim(device, put):
        turn = mirrored(device)
        if nd == 2:
            sides = [(1 - device, 0, 2 * LOOK)]
        else:
            sides = [(jnp.maximum(device - 1, 0), 0, LOOK), (jnp.minimum(device + 1, nd - 1), LOOK, 2 * LOOK)]
        for comp in range(2):
            cells = []
            for j in range(SUB):
                cell = zero
                for g in range(groups):
                    d = g * SUB + j
                    d = jnp.where(turn, local - 1 - d, d)
                    first = slot * g
                    for block, low, high in sides:
                        column = pl.ds(pl.multiple_of(block * width, width), width)
                        moved = pltpu.roll(x_ref[comp, d, :, column], (first + LOOK) % width, 1)
                        cell = jnp.where((lane >= first + low) & (lane < first + high), moved, cell)
                cells.append(cell)
            put(comp, turned(cells))

    own = place(me, me)

    def put_own(comp, near, tile):
        begin = pl.multiple_of(SUB + own * local + near.start, SUB)
        main[comp, pl.ds(LOOK, rows), pl.ds(begin, SUB)] = tile

    def put_own_rim(comp, tile):
        rim[own, comp, pl.ds(LOOK, rows), pl.ds(SUB, SUB)] = tile

    pack_rim(me, put_own_rim)
    pack(me, put_own)
    for k in range(1, nd):
        there = lax.rem(me + k, nd)

        def put_rim(comp, tile, k=k):
            packed_rim[k - 1, comp] = tile

        def put_main(comp, near, tile, k=k):
            packed[k - 1, comp, :, near] = tile

        pack_rim(there, put_rim)
        pack(there, put_main)

    pl.semaphore_wait(barrier, nd - 1 + has_up.astype(jnp.int32) + has_down.astype(jnp.int32))
    for n in range(parts + 1):
        for k in range(1, nd):
            give(k, n).start()
        start_halos(own, n, n == 0)

    inner = lax.broadcasted_iota(jnp.int32, (width, width), 0)
    outer = lax.broadcasted_iota(jnp.int32, (width, width), 1)
    box = (jnp.abs(inner - outer) <= LOOK).astype(jnp.float32).astype(jnp.bfloat16)
    for g in range(groups):
        cell = inner - slot * g
        left = (cell >= 0) & (cell < LOOK) & (outer <= cell) & (me > 0)
        right = (cell >= LOOK) & (cell < 2 * LOOK) & (outer >= width + cell - 2 * LOOK) & (me < nd - 1)
        edge = (left | right).astype(jnp.float32).astype(jnp.bfloat16)
        for begin, part in ((0, box), (1, box), (2, edge), (3, edge)):
            table[g, pl.ds(begin * width, width)] = part

    turn = mirrored(me)
    inner = lax.broadcasted_iota(jnp.int32, (dates, dates), 0)
    outer = lax.broadcasted_iota(jnp.int32, (dates, dates), 1)
    order = (inner == jnp.where(turn, dates - 1 - outer, outer)).astype(jnp.float32).astype(jnp.bfloat16)
    mask = jnp.transpose(net_ref[...].astype(jnp.float32), (1, 0)).astype(jnp.bfloat16)
    used_at[pl.ds(0, SUB)] = jnp.zeros((SUB, band), jnp.float32)
    used_at[pl.ds(SUB, dates)] = jnp.dot(order, mask, preferred_element_type=jnp.float32)

    for k in range(rows):
        root[k, pl.ds(0, SUB)] = blank
    for comp in range(2):
        for step in range(ITERS):
            for d in range(band):
                vec[step, comp, dates + d] = zero
    for step in range(ITERS):
        tot[step] = zero
        for c in range(3):
            for d in range(band):
                acc[step, c, d] = zero
    for c in range(3):
        for o in range(band):
            gam[c, o, pl.ds(dates * rows, band * rows)] = jnp.zeros((band * rows, width), jnp.float32)

    if nd != 2:
        for n in range(parts + 1):
            for k in range(1, nd):
                forward(k, n)

    lane = lax.broadcasted_iota(jnp.int32, (SUB, width), 1)

    def rim_sums(slab):
        before = jnp.maximum(slab - 1, 0)
        for comp in range(2):
            for r in range(tall):
                earlier = pltpu.roll(rim[slab, comp, r, pl.ds(SUB, SUB)], slot % width, 1)
                last = pltpu.roll(rim[before, comp, r, pl.ds(SUB, SUB)], (width - slot * (groups - 1)) % width, 1)
                last = jnp.where(slab > 0, last, 0.0)
                rim[slab, comp, r, pl.ds(0, SUB)] = jnp.where(lane < slot, last, earlier)

        def load(comp, r, offset):
            return rim[slab, comp, r, pl.ds(SUB - offset, SUB)]

        begin = 0
        for offset in range(band + 1):
            maps = halves(products(load, offset, tall))
            rim_maps[pl.ds(begin, maps.shape[0])] = maps
            begin += maps.shape[0]

    def tile_sums(t):
        g = lax.rem(t, groups)
        base = t * SUB
        here = pl.ds(pl.multiple_of(base + SUB, SUB), SUB)

        def load(comp, r, offset):
            return main[comp, r, here if offset == 0 else pl.ds(base + SUB - offset, SUB)]

        begin = 0
        for offset in range(band + 1):
            maps = halves(products(load, offset, tall))
            count = maps.shape[0]
            maps = jnp.concatenate([maps, rim_maps[pl.ds(begin, count)]], axis=1)
            begin += count
            sums = jnp.dot(maps, table[g], preferred_element_type=jnp.float32)
            if offset == 0:
                for k in range(rows):
                    root[k, here] = lax.rsqrt(sums[k * SUB : (k + 1) * SUB] + EPS)
                continue
            used = used_at[pl.ds(base + SUB - jnp.where(turn, 0, offset), SUB), :]
            used = used[:, offset - 1 : offset]
            for k in range(rows):
                weight = root[k, here] * root[k, pl.ds(base + SUB - offset, SUB)]
                weight = weight * used
                at = pl.ds((band + base - offset) * rows + k, SUB, stride=rows)
                c_re = sums[k * SUB : (k + 1) * SUB] * weight
                c_im = sums[(rows + k) * SUB : (rows + k + 1) * SUB] * weight
                gam[0, offset - 1, at] = c_re
                gam[1, offset - 1, at] = c_re + c_im
                gam[2, offset - 1, at] = c_im - c_re

    def at_date(d):
        return pl.ds(pl.multiple_of((band + d) * rows, rows), rows)

    def first(j):
        back_re = [acc[0, 0, i] for i in range(band)]
        back_sum = [acc[0, 1, i] for i in range(band)]
        total = tot[0]
        for i in range(SUB):
            d = j * SUB + i
            y_re = back_re[i] + 1.0
            y_im = back_re[i] - back_sum[i]
            ahead_re = ahead_sum = None
            for o in range(1, band + 1):
                c_re = gam[0, o - 1, at_date(d)]
                c_sum = gam[1, o - 1, at_date(d)]
                ahead_re = c_re if ahead_re is None else ahead_re + c_re
                ahead_sum = c_sum if ahead_sum is None else ahead_sum + c_sum
                if o == band:
                    back_re.append(c_re)
                    back_sum.append(c_sum)
                else:
                    back_re[i + o] = back_re[i + o] + c_re
                    back_sum[i + o] = back_sum[i + o] + c_sum
            y_re = y_re + ahead_re
            y_im = y_im + (ahead_sum - ahead_re)
            vec[0, 0, d] = y_re
            vec[0, 1, d] = y_im
            total = total + (y_re * y_re + y_im * y_im)
        for i in range(band):
            acc[0, 0, i] = back_re[SUB + i]
            acc[0, 1, i] = back_sum[SUB + i]
        tot[0] = total

    def later(step, j):
        acc_a, acc_b, acc_c = [[acc[step, c, i] for i in range(band)] for c in range(3)]
        base = j * SUB
        v_re = [vec[step - 1, 0, base + i] for i in range(band)]
        v_im = [vec[step - 1, 1, base + i] for i in range(band)]
        v_sum = [a + b for a, b in zip(v_re, v_im)]
        total = tot[step]
        for i in range(SUB):
            d = base + i
            v_re.append(vec[step - 1, 0, d + band])
            v_im.append(vec[step - 1, 1, d + band])
            v_sum.append(v_re[-1] + v_im[-1])
            y_a, y_b, y_c = acc_a[i], -acc_b[i], -acc_c[i]
            for o in range(1, band + 1):
                c_re = gam[0, o - 1, at_date(d)]
                c_sum = gam[1, o - 1, at_date(d)]
                c_dif = gam[2, o - 1, at_date(d)]
                y_a = y_a + c_re * v_sum[i + o]
                y_b = y_b + c_dif * v_re[i + o]
                y_c = y_c + c_sum * v_im[i + o]
                back_a = c_re * v_sum[i]
                back_b = c_sum * v_re[i]
                back_c = c_dif * v_im[i]
                if o == band:
                    acc_a.append(back_a)
                    acc_b.append(back_b)
                    acc_c.append(back_c)
                else:
                    acc_a[i + o] = acc_a[i + o] + back_a
                    acc_b[i + o] = acc_b[i + o] + back_b
                    acc_c[i + o] = acc_c[i + o] + back_c
            y_re = v_re[i] + (y_a - y_c)
            y_im = v_im[i] + (y_a + y_b)
            vec[step, 0, d] = y_re
            vec[step, 1, d] = y_im
            total = total + (y_re * y_re + y_im * y_im)
        for i in range(band):
            acc[step, 0, i] = acc_a[SUB + i]
            acc[step, 1, i] = acc_b[SUB + i]
            acc[step, 2, i] = acc_c[SUB + i]
        tot[step] = total

    def advance(t, carry):
        if nd == 2:
            for n in range(parts + 1):

                @pl.when(t == (groups * 5 * n) // (4 * parts))
                def _(n=n):
                    forward(1, n)

        @pl.when(t < tiles)
        def _():
            slab = lax.div(t, groups)
            g = lax.rem(t, groups)

            @pl.when(lax.rem(g, span) == 0)
            def _():
                await_halos(slab, 1 + lax.div(g, span), False)

            @pl.when(g == 0)
            def _():
                await_halos(slab, 0, True)
                rim_sums(slab)

            tile_sums(t)

        @pl.when((t >= 1) & (t <= tiles))
        def _():
            first(t - 1)

        def level(step, carry):
            later(step, t - 1 - step)
            return carry

        lax.fori_loop(jnp.maximum(1, t - tiles), jnp.minimum(t, ITERS), level, 0)
        return carry

    lax.fori_loop(0, tiles + ITERS, advance, 0)

    for n in range(parts + 1):
        for k in range(1, nd):
            give(k, n).wait_send()
        for s in range(nd):

            @pl.when(has_up)
            def _():
                halo(s, n, True, n == 0).wait_send()

            @pl.when(has_down)
            def _():
                halo(s, n, False, n == 0).wait_send()


def scale_kernel(nd, vec, tot, out_ref):
    dates = out_ref.shape[1]
    scale = None
    for step in range(ITERS):
        mean = tot[step] / dates
        if scale is None:
            scale = lax.rsqrt(mean + EPS)
        else:
            scale = scale * lax.rsqrt(scale * scale * mean + EPS)
    turn = 2 * lax.axis_index("date") >= nd

    def block(b, carry):
        for j in range(SUB):
            d = b * SUB + j
            at = jnp.where(turn, dates - 1 - d, d)
            for comp in range(2):
                out_ref[comp, at] = vec[ITERS - 1, comp, d] * scale
        return carry

    lax.fori_loop(0, dates // SUB, block, 0)


def on_device(nd, nr, slc, network):
    _, local, rows, cols = slc.shape
    width = cols // nd
    dates, band = network.shape
    tall = rows + 2 * LOOK
    maps = (2 * band + 1) * rows * SUB
    parts = local // CHUNK if local % CHUNK == 0 else 1
    whole = pl.BlockSpec(memory_space=pltpu.VMEM)
    away = pl.BlockSpec(memory_space=pltpu.HBM)
    f32 = jnp.float32
    give_sems = pltpu.SemaphoreType.DMA((nd, parts + 1))
    vec, tot = pl.pallas_call(
        functools.partial(main_kernel, nd, nr),
        out_shape=[
            pltpu.VMEM((ITERS, 2, dates + band, rows, width), f32),
            pltpu.VMEM((ITERS, rows, width), f32),
        ],
        in_specs=[away, whole],
        out_specs=[whole, whole],
        scratch_shapes=[
            pltpu.VMEM((2, local, rows, cols), f32),
            pltpu.VMEM((nd - 1, 2, rows, local, width), f32),
            pltpu.VMEM((nd - 1, 2, rows, SUB, width), f32),
            pltpu.VMEM((2, tall, SUB + dates, width), f32),
            pltpu.VMEM((nd, 2, tall, 2 * SUB, width), f32),
            pltpu.VMEM((maps, 2 * width), jnp.bfloat16),
            pltpu.VMEM((local // SUB, 4 * width, width), jnp.bfloat16),
            pltpu.VMEM((rows, SUB + dates, width), f32),
            pltpu.VMEM((SUB + dates, band), f32),
            pltpu.VMEM((3, band, (band + dates) * rows, width), f32),
            pltpu.VMEM((ITERS, 3, band, rows, width), f32),
            pltpu.SemaphoreType.DMA(()),
        ]
        + [give_sems] * 6,
        compiler_params=pltpu.CompilerParams(
            collective_id=0, has_side_effects=True, vmem_limit_bytes=40 * 1024 * 1024
        ),
        name="link",
    )(pltpu.with_memory_space_constraint(slc, pltpu.HBM), network.T)
    vec = pltpu.with_memory_space_constraint(vec, pltpu.VMEM)
    tot = pltpu.with_memory_space_constraint(tot, pltpu.VMEM)
    return pl.pallas_call(
        functools.partial(scale_kernel, nd),
        out_shape=jax.ShapeDtypeStruct((2, dates, rows, width), f32),
        in_specs=[whole, whole],
        out_specs=whole,
        compiler_params=pltpu.CompilerParams(vmem_limit_bytes=8 * 1024 * 1024),
        name="scale",
    )(vec, tot)


def solution(mesh):
    return jax.shard_map(
        functools.partial(on_device, mesh.shape["date"], mesh.shape["row"]),
        mesh=mesh,
        in_specs=(P(None, "date", "row", None), P()),
        out_specs=P(None, None, "row", "date"),
        check_vma=False,
    )
```

```python
import functools

import jax
import jax.numpy as jnp
from jax import lax
from jax.experimental import pallas as pl
from jax.experimental.pallas import tpu as pltpu
from jax.sharding import PartitionSpec as P

LOOK = 5
ITERS = 5
SUB = 8
PIECE = 16
AHEAD = 3
STRIDE = 2
EPS = 1e-06
MESH = pl.DeviceIdType.MESH


def row_sums(cells):
    span = 2 * LOOK + 1
    count = len(cells) - span + 1
    head = functools.reduce(jnp.add, cells[count - 1 : span])
    heads = [head]
    for k in range(count - 2, -1, -1):
        heads.append(heads[-1] + cells[k])
    heads = heads[::-1]
    sums = [heads[0]]
    tail = None
    for k in range(1, count):
        cell = cells[span + k - 1]
        tail = cell if tail is None else tail + cell
        sums.append(heads[k] + tail)
    return sums


def halves(sums):
    stacked = jnp.concatenate(sums, axis=0)
    high = stacked.astype(jnp.bfloat16)
    low = (stacked - high.astype(jnp.float32)).astype(jnp.bfloat16)
    return jnp.concatenate([high, low], axis=1)


def main_kernel(
    nd, nr, x_hbm, net_ref, vec, tot,
    x_ref, stack, main, rim_maps, box, edges, root, used_at, gam, acc, load_sem,
    give_send, give_recv, up_send, up_recv, down_send, down_recv,
):
    _, local, rows, _ = x_ref.shape
    width = main.shape[3]
    band, dates = net_ref.shape
    groups = local // SUB
    slot = width // groups
    tiles = dates // SUB
    tall = rows + 2 * LOOK
    work = SUB + dates
    rims = work + 2 * SUB
    pad = 2 * band
    parts = give_send.shape[1] - 1
    piece = local // parts
    span = piece // SUB
    me = lax.axis_index("date")
    row = lax.axis_index("row")
    has_up = row > 0
    has_down = row < nr - 1
    up = jnp.maximum(row - 1, 0)
    down = jnp.minimum(row + 1, nr - 1)

    def mirrored(device):
        return 2 * device >= nd

    def place(source, device):
        return jnp.where(mirrored(device), nd - 1 - source, source)

    own = place(me, me)
    turn = mirrored(me)
    barrier = pltpu.get_barrier_semaphore()
    for k in range(1, nd):
        pl.semaphore_signal(barrier, 1, device_id=(lax.rem(me + k, nd), row), device_id_type=MESH)

    @pl.when(has_up)
    def _():
        pl.semaphore_signal(barrier, 1, device_id=(me, up), device_id_type=MESH)

    @pl.when(has_down)
    def _():
        pl.semaphore_signal(barrier, 1, device_id=(me, down), device_id_type=MESH)

    def aligned(start, size=SUB):
        return pl.ds(pl.multiple_of(start, SUB), size)

    def columns(device):
        return pl.ds(pl.multiple_of(device * width, width), width)

    fetch_own = pltpu.make_async_copy(x_hbm.at[:, :, :, columns(me)], stack.at[0], load_sem.at[0])
    fetch_own.start()
    fetch = pltpu.make_async_copy(x_hbm, x_ref, load_sem.at[1])
    fetch.start()

    def give(k, n):
        there = lax.rem(me + k, nd)
        near = pl.ds(jnp.where(mirrored(there), local - (n + 1) * piece, n * piece), piece)
        return pltpu.make_async_remote_copy(
            src_ref=x_hbm.at[:, near, :, columns(there)],
            dst_ref=stack.at[k, :, near],
            send_sem=give_send.at[k, n],
            recv_sem=give_recv.at[k, n],
            device_id=(there, row),
            device_id_type=MESH,
        )

    def give_rim(k):
        there = lax.rem(me + k, nd)
        inner = pl.ds(LOOK, rows)
        return pltpu.make_async_remote_copy(
            src_ref=main.at[:, inner, pl.ds(rims + (nd + k - 1) * SUB, SUB)],
            dst_ref=main.at[:, inner, aligned(rims + place(me, there) * SUB)],
            send_sem=give_send.at[k, parts],
            recv_sem=give_recv.at[k, parts],
            device_id=(there, row),
            device_id_type=MESH,
        )

    def halo(slab, n, to_up, size):
        near = aligned(rims + slab * SUB if n is parts else SUB + slab * local + n * piece, size)
        return pltpu.make_async_remote_copy(
            src_ref=main.at[:, pl.ds(LOOK if to_up else rows, LOOK), near],
            dst_ref=main.at[:, pl.ds(LOOK + rows if to_up else 0, LOOK), near],
            send_sem=(up_send if to_up else down_send).at[slab, n],
            recv_sem=(up_recv if to_up else down_recv).at[slab, n],
            device_id=(me, up if to_up else down),
            device_id_type=MESH,
        )

    def both_ways(slab, n, act):
        size = SUB if n is parts else piece

        @pl.when(has_up)
        def _():
            act(halo(slab, n, True, size), halo(slab, n, False, size))

        @pl.when(has_down)
        def _():
            act(halo(slab, n, False, size), halo(slab, n, True, size))

    def start_halos(slab, n):
        both_ways(slab, n, lambda there, back: there.start())

    def await_halos(slab, n):
        both_ways(slab, n, lambda there, back: back.wait_recv())

    def await_sent(slab, n):
        both_ways(slab, n, lambda there, back: there.wait_send())

    def slab_of(k):
        return place(lax.rem(me + nd - k, nd), me)

    def turned(cells):
        return jnp.transpose(jnp.stack(cells), (1, 0, 2))

    def take(k, n):
        slab = slab_of(k)
        for s in range(span):
            for comp in range(2):
                cells = []
                for j in range(SUB):
                    d = n * piece + s * SUB + j
                    cells.append(stack[k, comp, jnp.where(turn, local - 1 - d, d)])
                at = SUB + slab * local + n * piece + s * SUB
                main[comp, pl.ds(LOOK, rows), aligned(at)] = turned(cells)
        start_halos(slab, n)

    zero = jnp.zeros((rows, width), jnp.float32)
    blank = jnp.zeros((SUB, width), jnp.float32)
    lane = lax.broadcasted_iota(jnp.int32, (rows, width), 1)

    def pack_rim(k, carry):
        device = lax.rem(me + k, nd)
        back = mirrored(device)
        at = rims + jnp.where(k == 0, own, nd + k - 1) * SUB
        if nd == 2:
            sides = [(1 - device, 0, 2 * LOOK)]
        else:
            sides = [(jnp.maximum(device - 1, 0), 0, LOOK), (jnp.minimum(device + 1, nd - 1), LOOK, 2 * LOOK)]

        def group(g, cells):
            cells = list(cells)
            begin = slot * g
            for comp in range(2):
                for j in range(SUB):
                    d = g * SUB + j
                    d = jnp.where(back, local - 1 - d, d)
                    i = comp * SUB + j
                    for block, low, high in sides:
                        moved = pltpu.roll(x_ref[comp, d, :, columns(block)], begin + LOOK, 1)
                        cells[i] = jnp.where((lane >= begin + low) & (lane < begin + high), moved, cells[i])
            return tuple(cells)

        cells = lax.fori_loop(0, groups, group, tuple(zero for _ in range(2 * SUB)), unroll=2)
        for comp in range(2):
            main[comp, pl.ds(LOOK, rows), aligned(at)] = turned(cells[comp * SUB : (comp + 1) * SUB])
        return carry

    def clear_rows(begin):
        def clear(i, carry):
            main[lax.rem(i, 2), begin + lax.div(i, 2), pl.ds(0, rims + nd * SUB)] = jnp.zeros((rims + nd * SUB, width), jnp.float32)
            return carry

        lax.fori_loop(0, 2 * LOOK, clear, 0)

    @pl.when(jnp.logical_not(has_up))
    def _():
        clear_rows(0)

    @pl.when(jnp.logical_not(has_down))
    def _():
        clear_rows(LOOK + rows)

    def clear_front(r, carry):
        for comp in range(2):
            main[comp, r, pl.ds(0, SUB)] = blank
            main[comp, r, pl.ds(work + SUB, SUB)] = blank
        return carry

    lax.fori_loop(0, tall, clear_front, 0)
    pl.semaphore_wait(barrier, nd - 1 + has_up.astype(jnp.int32) + has_down.astype(jnp.int32))
    for k in range(1, nd):
        give(k, 0).start()
    fetch_own.wait()

    def send(n, carry):
        take(0, n)

        @pl.when(n == 0)
        def _():
            fetch.wait()
            lax.fori_loop(0, nd, pack_rim, 0)
            start_halos(own, parts)
            for k in range(1, nd):
                give_rim(k).start()

        @pl.when(n > 0)
        def _():
            for k in range(1, nd):
                give(k, n).start()

        return carry

    lax.fori_loop(0, parts, send, 0)

    inner = lax.broadcasted_iota(jnp.int32, (width, width), 0)
    outer = lax.broadcasted_iota(jnp.int32, (width, width), 1)
    near = (jnp.abs(inner - outer) <= LOOK).astype(jnp.float32).astype(jnp.bfloat16)
    box[pl.ds(0, width)] = near
    box[pl.ds(width, width)] = near

    def edge_table(g, carry):
        cell = inner - slot * g
        left = (cell >= 0) & (cell < LOOK) & (outer <= cell) & (me > 0)
        right = (cell >= LOOK) & (cell < 2 * LOOK) & (outer >= width + cell - 2 * LOOK) & (me < nd - 1)
        edge = (left | right).astype(jnp.float32).astype(jnp.bfloat16)
        edges[g, pl.ds(0, width)] = edge
        edges[g, pl.ds(width, width)] = edge
        return carry

    lax.fori_loop(0, groups, edge_table, 0)
    inner = lax.broadcasted_iota(jnp.int32, (dates, dates), 0)
    outer = lax.broadcasted_iota(jnp.int32, (dates, dates), 1)
    order = (inner == jnp.where(turn, dates - 1 - outer, outer)).astype(jnp.float32).astype(jnp.bfloat16)
    mask = jnp.transpose(net_ref[...].astype(jnp.float32), (1, 0)).astype(jnp.bfloat16)
    mask = jnp.dot(order, mask, preferred_element_type=jnp.float32)

    def spread(o, carry):
        column = lax.broadcasted_iota(jnp.int32, (dates, band), 1) == o
        column = jnp.sum(jnp.where(column, mask, 0.0), axis=1, keepdims=True)
        used_at[o, pl.ds(0, pad)] = jnp.zeros((pad, width), jnp.float32)
        used_at[o, pl.ds(pad, dates)] = jnp.broadcast_to(column, (dates, width))
        return carry

    lax.fori_loop(0, band, spread, 0)
    for k in range(rows):
        root[k, pl.ds(0, pad)] = jnp.zeros((pad, width), jnp.float32)

    def clear_state(step, carry):
        for d in range(band):
            for comp in range(2):
                vec[step, comp, dates + d] = zero
            for c in range(3):
                acc[step, c, d] = zero
        tot[step] = zero
        return carry

    lax.fori_loop(0, ITERS, clear_state, 0)

    def clear_last(o, carry):
        for c in range(3):
            for d in range(band):
                gam[c, o, pl.ds((pad + dates - band + d) * rows, rows)] = zero
        return carry

    lax.fori_loop(0, band, clear_last, 0)

    def forward_rim(k):
        give_rim(k).wait_recv()
        start_halos(slab_of(k), parts)

    def forward(k, n):
        give(k, n).wait_recv()
        take(k, n)

    if nd != 2:
        for k in range(1, nd):
            forward_rim(k)
            for n in range(parts):
                forward(k, n)

    lane = lax.broadcasted_iota(jnp.int32, (SUB, width), 1)

    def open_slab(slab):
        def part(comp, carry):
            here = [main[comp, r, aligned(rims + slab * SUB)] for r in range(tall)]
            last = [main[comp, r, pl.ds(work + SUB, SUB)] for r in range(tall)]
            earlier = [pltpu.roll(cell, slot % width, 1) for cell in here]
            last = [pltpu.roll(cell, (width - slot * (groups - 1)) % width, 1) for cell in last]
            for r in range(tall):
                main[comp, r, pl.ds(work, SUB)] = jnp.where(lane < slot, last[r], earlier[r])
                main[comp, r, pl.ds(work + SUB, SUB)] = here[r]
            return carry

        lax.fori_loop(0, 2, part, 0)

    def pair_rows(o, base):
        part_re, part_im = [], []
        here, ahead = aligned(base), pl.ds(base - o, SUB)
        for r in range(tall):
            a_re, a_im = main[0, r, ahead], main[1, r, ahead]
            b_re, b_im = main[0, r, here], main[1, r, here]
            part_re.append(a_re * b_re + a_im * b_im)
            part_im.append(a_im * b_re - a_re * b_im)
        return halves(row_sums(part_re) + row_sums(part_im))

    each = 2 * rows * SUB

    def rim_sums():
        base = work + SUB
        rim_maps[pl.ds(0, each // 2)] = square_rows(base)

        def offset(o, carry):
            begin = pl.multiple_of(each // 2 + (o - 1) * each, each // 2)
            rim_maps[pl.ds(begin, each)] = pair_rows(o, base)
            return carry

        lax.fori_loop(1, band + 1, offset, 0)

    def square_rows(base):
        squares = []
        for r in range(tall):
            re, im = main[0, r, aligned(base)], main[1, r, aligned(base)]
            squares.append(re * re + im * im)
        return halves(row_sums(squares))

    def tile_sums(t):
        g = lax.rem(t, groups)
        base = SUB + t * SUB
        to = pad + t * SUB
        here = aligned(to)

        def column_sums(rows_of, begin):
            rim = rim_maps[pl.ds(begin, rows_of.shape[0])]
            table = jnp.concatenate([box[...], edges[g]], axis=0)
            return jnp.dot(jnp.concatenate([rows_of, rim], axis=1), table, preferred_element_type=jnp.float32)

        power = lax.rsqrt(column_sums(square_rows(base), 0) + EPS)
        for k in range(rows):
            root[k, here] = power[k * SUB : (k + 1) * SUB]
        for i in range(0, band, STRIDE):
            begin = each // 2 + i * each
            sums = column_sums(jnp.concatenate([pair_rows(i + s + 1, base) for s in range(STRIDE)], axis=0), begin)
            for s in range(STRIDE):
                o = i + s + 1
                used = used_at[o - 1, pl.ds(jnp.where(turn, to, to - o), SUB)]
                for k in range(rows):
                    weight = root[k, here] * root[k, pl.ds(to - o, SUB)] * used
                    at = pl.ds((to - o) * rows + k, SUB, stride=rows)
                    c_re = sums[s * each + k * SUB : s * each + (k + 1) * SUB] * weight
                    c_im = sums[s * each + (rows + k) * SUB : s * each + (rows + k + 1) * SUB] * weight
                    gam[0, o - 1, at] = c_re
                    gam[1, o - 1, at] = c_re + c_im
                    gam[2, o - 1, at] = c_im - c_re

    def at_date(d):
        return pl.ds(pl.multiple_of((pad + d) * rows, rows), rows)

    def first(j):
        back_re = [acc[0, 0, i] for i in range(band)]
        back_sum = [acc[0, 1, i] for i in range(band)]
        total = tot[0]
        for i in range(SUB):
            d = j * SUB + i
            y_re = back_re[i] + 1.0
            y_im = back_re[i] - back_sum[i]
            ahead_re = ahead_sum = None
            for o in range(1, band + 1):
                c_re = gam[0, o - 1, at_date(d)]
                c_sum = gam[1, o - 1, at_date(d)]
                ahead_re = c_re if ahead_re is None else ahead_re + c_re
                ahead_sum = c_sum if ahead_sum is None else ahead_sum + c_sum
                if o == band:
                    back_re.append(c_re)
                    back_sum.append(c_sum)
                else:
                    back_re[i + o] = back_re[i + o] + c_re
                    back_sum[i + o] = back_sum[i + o] + c_sum
            y_re = y_re + ahead_re
            y_im = y_im + (ahead_sum - ahead_re)
            vec[0, 0, d] = y_re
            vec[0, 1, d] = y_im
            total = total + (y_re * y_re + y_im * y_im)
        for i in range(band):
            acc[0, 0, i] = back_re[SUB + i]
            acc[0, 1, i] = back_sum[SUB + i]
        tot[0] = total

    def later(step, j):
        acc_a, acc_b, acc_c = [[acc[step, c, i] for i in range(band)] for c in range(3)]
        base = j * SUB
        v_re = [vec[step - 1, 0, base + i] for i in range(band)]
        v_im = [vec[step - 1, 1, base + i] for i in range(band)]
        v_sum = [a + b for a, b in zip(v_re, v_im)]
        total = tot[step]
        for i in range(SUB):
            d = base + i
            v_re.append(vec[step - 1, 0, d + band])
            v_im.append(vec[step - 1, 1, d + band])
            v_sum.append(v_re[-1] + v_im[-1])
            y_a, y_b, y_c = acc_a[i], -acc_b[i], -acc_c[i]
            for o in range(1, band + 1):
                c_re = gam[0, o - 1, at_date(d)]
                c_sum = gam[1, o - 1, at_date(d)]
                c_dif = gam[2, o - 1, at_date(d)]
                y_a = y_a + c_re * v_sum[i + o]
                y_b = y_b + c_dif * v_re[i + o]
                y_c = y_c + c_sum * v_im[i + o]
                back_a = c_re * v_sum[i]
                back_b = c_sum * v_re[i]
                back_c = c_dif * v_im[i]
                if o == band:
                    acc_a.append(back_a)
                    acc_b.append(back_b)
                    acc_c.append(back_c)
                else:
                    acc_a[i + o] = acc_a[i + o] + back_a
                    acc_b[i + o] = acc_b[i + o] + back_b
                    acc_c[i + o] = acc_c[i + o] + back_c
            y_re = v_re[i] + (y_a - y_c)
            y_im = v_im[i] + (y_a + y_b)
            vec[step, 0, d] = y_re
            vec[step, 1, d] = y_im
            total = total + (y_re * y_re + y_im * y_im)
        for i in range(band):
            acc[step, 0, i] = acc_a[SUB + i]
            acc[step, 1, i] = acc_b[SUB + i]
            acc[step, 2, i] = acc_c[SUB + i]
        tot[step] = total

    def advance(t, carry):
        if nd == 2:

            @pl.when(t == 1)
            def _():
                forward_rim(1)

            @pl.when((lax.rem(t, AHEAD) == 1) & (t < AHEAD * parts))
            def _():
                forward(1, lax.div(t, AHEAD))

        @pl.when(t < tiles)
        def _():
            slab, g = lax.div(t, groups), lax.rem(t, groups)

            @pl.when(g == 0)
            def _():
                await_halos(slab, parts)
                open_slab(slab)
                rim_sums()

            @pl.when(lax.rem(g, span) == 0)
            def _():
                await_halos(slab, lax.div(g, span))

            tile_sums(t)

        @pl.when((t >= 1) & (t <= tiles))
        def _():
            first(t - 1)

        def level(step, carry):
            later(step, t - 1 - step)
            return carry

        lax.fori_loop(jnp.maximum(1, t - tiles), jnp.minimum(t, ITERS), level, 0)
        return carry

    lax.fori_loop(0, tiles + ITERS, advance, 0)

    def sent(n, carry):
        for k in range(1, nd):
            give(k, n).wait_send()
        for s in range(nd):
            await_sent(s, n)
        return carry

    lax.fori_loop(0, parts, sent, 0)
    for k in range(1, nd):
        give_rim(k).wait_send()
    for s in range(nd):
        await_sent(s, parts)


def scale_kernel(nd, vec, tot, out_ref):
    dates = out_ref.shape[1]
    scale = None
    for step in range(ITERS):
        mean = tot[step] / dates
        if scale is None:
            scale = lax.rsqrt(mean + EPS)
        else:
            scale = scale * lax.rsqrt(scale * scale * mean + EPS)
    turn = 2 * lax.axis_index("date") >= nd

    def block(b, carry):
        for j in range(SUB):
            d = b * SUB + j
            at = jnp.where(turn, dates - 1 - d, d)
            for comp in range(2):
                out_ref[comp, at] = vec[ITERS - 1, comp, d] * scale
        return carry

    lax.fori_loop(0, dates // SUB, block, 0)


def on_device(nd, nr, slc, network):
    _, local, rows, cols = slc.shape
    width = cols // nd
    dates, band = network.shape
    tall = rows + 2 * LOOK
    maps = (2 * band + 1) * rows * SUB
    parts = local // PIECE if local % PIECE == 0 else 1
    whole = pl.BlockSpec(memory_space=pltpu.VMEM)
    away = pl.BlockSpec(memory_space=pltpu.HBM)
    f32, bf16 = jnp.float32, jnp.bfloat16
    sems = pltpu.SemaphoreType.DMA((nd, parts + 1))
    vec, tot = pl.pallas_call(
        functools.partial(main_kernel, nd, nr),
        out_shape=[
            pltpu.VMEM((ITERS, 2, dates + band, rows, width), f32),
            pltpu.VMEM((ITERS, rows, width), f32),
        ],
        in_specs=[away, whole],
        out_specs=[whole, whole],
        scratch_shapes=[
            pltpu.VMEM((2, local, rows, cols), f32),
            pltpu.VMEM((nd, 2, local, rows, width), f32),
            pltpu.VMEM((2, tall, dates + (2 * nd + 2) * SUB, width), f32),
            pltpu.VMEM((maps, 2 * width), bf16),
            pltpu.VMEM((2 * width, width), bf16),
            pltpu.VMEM((local // SUB, 2 * width, width), bf16),
            pltpu.VMEM((rows, 2 * band + dates, width), f32),
            pltpu.VMEM((band, 2 * band + dates, width), f32),
            pltpu.VMEM((3, band, (2 * band + dates) * rows, width), f32),
            pltpu.VMEM((ITERS, 3, band, rows, width), f32),
            pltpu.SemaphoreType.DMA((2,)),
        ]
        + [sems] * 6,
        compiler_params=pltpu.CompilerParams(
            collective_id=0, has_side_effects=True, vmem_limit_bytes=40 * 1024 * 1024
        ),
        name="link",
    )(pltpu.with_memory_space_constraint(slc, pltpu.HBM), network.T)
    vec = pltpu.with_memory_space_constraint(vec, pltpu.VMEM)
    tot = pltpu.with_memory_space_constraint(tot, pltpu.VMEM)
    return pl.pallas_call(
        functools.partial(scale_kernel, nd),
        out_shape=jax.ShapeDtypeStruct((2, dates, rows, width), f32),
        in_specs=[whole, whole],
        out_specs=whole,
        compiler_params=pltpu.CompilerParams(vmem_limit_bytes=8 * 1024 * 1024),
        name="scale",
    )(vec, tot)


def solution(mesh):
    return jax.shard_map(
        functools.partial(on_device, mesh.shape["date"], mesh.shape["row"]),
        mesh=mesh,
        in_specs=(P(None, "date", "row", None), P()),
        out_specs=P(None, None, "row", "date"),
        check_vma=False,
    )
```

```python
import functools

import jax
import jax.numpy as jnp
from jax import lax
from jax.experimental import pallas as pl
from jax.experimental.pallas import tpu as pltpu
from jax.sharding import PartitionSpec as P

LOOK = 5
ITERS = 5
SUB = 8
PIECE = 8
AHEAD = 3
FIRST = 3
EDGES = 4
STRIDE = 2
EPS = 1e-06
MESH = pl.DeviceIdType.MESH


def row_sums(cells):
    span = 2 * LOOK + 1
    count = len(cells) - span + 1
    head = functools.reduce(jnp.add, cells[count - 1 : span])
    heads = [head]
    for k in range(count - 2, -1, -1):
        heads.append(heads[-1] + cells[k])
    heads = heads[::-1]
    sums = [heads[0]]
    tail = None
    for k in range(1, count):
        cell = cells[span + k - 1]
        tail = cell if tail is None else tail + cell
        sums.append(heads[k] + tail)
    return sums


def halves(sums):
    stacked = jnp.concatenate(sums, axis=0)
    high = stacked.astype(jnp.bfloat16)
    low = (stacked - high.astype(jnp.float32)).astype(jnp.bfloat16)
    return jnp.concatenate([high, low], axis=1)


def main_kernel(
    nd, nr, x_hbm, net_hbm, vec, tot,
    net_ref, x_ref, stack, main, rim_maps, box, edges, root, used_at, gam, acc, load_sem,
    give_send, give_recv, up_send, up_recv, down_send, down_recv,
):
    _, local, rows, _ = x_ref.shape
    width = main.shape[3]
    band, dates = net_ref.shape
    groups = local // SUB
    slot = width // groups
    tiles = dates // SUB
    tall = rows + 2 * LOOK
    work = SUB + dates
    rims = work + 2 * SUB
    pad = 2 * band
    parts = give_send.shape[1] - 1
    piece = local // parts
    span = piece // SUB
    me = lax.axis_index("date")
    row = lax.axis_index("row")
    has_up = row > 0
    has_down = row < nr - 1
    up = jnp.maximum(row - 1, 0)
    down = jnp.minimum(row + 1, nr - 1)

    def mirrored(device):
        return 2 * device >= nd

    def place(source, device):
        return jnp.where(mirrored(device), nd - 1 - source, source)

    own = place(me, me)
    turn = mirrored(me)
    barrier = pltpu.get_barrier_semaphore()
    for k in range(1, nd):
        pl.semaphore_signal(barrier, 1, device_id=(lax.rem(me + k, nd), row), device_id_type=MESH)

    @pl.when(has_up)
    def _():
        pl.semaphore_signal(barrier, 1, device_id=(me, up), device_id_type=MESH)

    @pl.when(has_down)
    def _():
        pl.semaphore_signal(barrier, 1, device_id=(me, down), device_id_type=MESH)

    def aligned(start, size=SUB):
        return pl.ds(pl.multiple_of(start, SUB), size)

    def columns(device):
        return pl.ds(pl.multiple_of(device * width, width), width)

    fetch_own = pltpu.make_async_copy(x_hbm.at[:, :, :, columns(me)], stack.at[0], load_sem.at[0])
    fetch_own.start()
    fetch = pltpu.make_async_copy(x_hbm, x_ref, load_sem.at[1])
    fetch.start()
    fetch_net = pltpu.make_async_copy(net_hbm, net_ref, load_sem.at[2])
    fetch_net.start()

    def give(k, n):
        there = lax.rem(me + k, nd)
        near = pl.ds(jnp.where(mirrored(there), local - (n + 1) * piece, n * piece), piece)
        return pltpu.make_async_remote_copy(
            src_ref=x_hbm.at[:, near, :, columns(there)],
            dst_ref=stack.at[k, :, near],
            send_sem=give_send.at[k, n],
            recv_sem=give_recv.at[k, n],
            device_id=(there, row),
            device_id_type=MESH,
        )

    def give_rim(k):
        there = lax.rem(me + k, nd)
        inner = pl.ds(LOOK, rows)
        return pltpu.make_async_remote_copy(
            src_ref=main.at[:, inner, pl.ds(rims + (nd + k - 1) * SUB, SUB)],
            dst_ref=main.at[:, inner, aligned(rims + place(me, there) * SUB)],
            send_sem=give_send.at[k, parts],
            recv_sem=give_recv.at[k, parts],
            device_id=(there, row),
            device_id_type=MESH,
        )

    def halo(slab, n, to_up, size):
        near = aligned(rims + slab * SUB if n is parts else SUB + slab * local + n * piece, size)
        return pltpu.make_async_remote_copy(
            src_ref=main.at[:, pl.ds(LOOK if to_up else rows, LOOK), near],
            dst_ref=main.at[:, pl.ds(LOOK + rows if to_up else 0, LOOK), near],
            send_sem=(up_send if to_up else down_send).at[slab, n],
            recv_sem=(up_recv if to_up else down_recv).at[slab, n],
            device_id=(me, up if to_up else down),
            device_id_type=MESH,
        )

    def both_ways(slab, n, act):
        size = SUB if n is parts else piece

        @pl.when(has_up)
        def _():
            act(halo(slab, n, True, size), halo(slab, n, False, size))

        @pl.when(has_down)
        def _():
            act(halo(slab, n, False, size), halo(slab, n, True, size))

    def start_halos(slab, n):
        both_ways(slab, n, lambda there, back: there.start())

    def await_halos(slab, n):
        both_ways(slab, n, lambda there, back: back.wait_recv())

    def await_sent(slab, n):
        both_ways(slab, n, lambda there, back: there.wait_send())

    def slab_of(k):
        return place(lax.rem(me + nd - k, nd), me)

    def turned(cells):
        return jnp.transpose(jnp.stack(cells), (1, 0, 2))

    def take(k, n):
        slab = slab_of(k)
        for s in range(span):
            for comp in range(2):
                cells = []
                for j in range(SUB):
                    d = n * piece + s * SUB + j
                    cells.append(stack[k, comp, jnp.where(turn, local - 1 - d, d)])
                at = SUB + slab * local + n * piece + s * SUB
                main[comp, pl.ds(LOOK, rows), aligned(at)] = turned(cells)
        start_halos(slab, n)

    zero = jnp.zeros((rows, width), jnp.float32)
    blank = jnp.zeros((SUB, width), jnp.float32)
    lane = lax.broadcasted_iota(jnp.int32, (rows, width), 1)

    def pack_rim(k, carry):
        device = lax.rem(me + k, nd)
        back = mirrored(device)
        at = rims + jnp.where(k == 0, own, nd + k - 1) * SUB
        if nd == 2:
            sides = [(1 - device, 0, 2 * LOOK)]
        else:
            sides = [(jnp.maximum(device - 1, 0), 0, LOOK), (jnp.minimum(device + 1, nd - 1), LOOK, 2 * LOOK)]

        def group(g, cells):
            cells = list(cells)
            begin = slot * g
            for comp in range(2):
                for j in range(SUB):
                    d = g * SUB + j
                    d = jnp.where(back, local - 1 - d, d)
                    i = comp * SUB + j
                    for block, low, high in sides:
                        moved = pltpu.roll(x_ref[comp, d, :, columns(block)], begin + LOOK, 1)
                        cells[i] = jnp.where((lane >= begin + low) & (lane < begin + high), moved, cells[i])
            return tuple(cells)

        cells = lax.fori_loop(0, groups, group, tuple(zero for _ in range(2 * SUB)), unroll=2)
        for comp in range(2):
            main[comp, pl.ds(LOOK, rows), aligned(at)] = turned(cells[comp * SUB : (comp + 1) * SUB])
        return carry

    def clear_rows(begin):
        def clear(i, carry):
            main[lax.rem(i, 2), begin + lax.div(i, 2), pl.ds(0, rims + nd * SUB)] = jnp.zeros((rims + nd * SUB, width), jnp.float32)
            return carry

        lax.fori_loop(0, 2 * LOOK, clear, 0)

    @pl.when(jnp.logical_not(has_up))
    def _():
        clear_rows(0)

    @pl.when(jnp.logical_not(has_down))
    def _():
        clear_rows(LOOK + rows)

    def clear_front(r, carry):
        for comp in range(2):
            main[comp, r, pl.ds(0, SUB)] = blank
            main[comp, r, pl.ds(work + SUB, SUB)] = blank
        return carry

    lax.fori_loop(0, tall, clear_front, 0)
    inner = lax.broadcasted_iota(jnp.int32, (width, width), 0)
    outer = lax.broadcasted_iota(jnp.int32, (width, width), 1)
    near = (jnp.abs(inner - outer) <= LOOK).astype(jnp.float32).astype(jnp.bfloat16)
    box[pl.ds(0, width)] = near
    box[pl.ds(width, width)] = near

    def edge_table(g, carry):
        cell = inner - slot * g
        left = (cell >= 0) & (cell < LOOK) & (outer <= cell) & (me > 0)
        right = (cell >= LOOK) & (cell < 2 * LOOK) & (outer >= width + cell - 2 * LOOK) & (me < nd - 1)
        edge = (left | right).astype(jnp.float32).astype(jnp.bfloat16)
        edges[g, pl.ds(0, width)] = edge
        edges[g, pl.ds(width, width)] = edge
        return carry

    lax.fori_loop(0, groups, edge_table, 0)
    for k in range(rows):
        root[k, pl.ds(0, pad)] = jnp.zeros((pad, width), jnp.float32)

    def clear_state(step, carry):
        for d in range(band):
            for comp in range(2):
                vec[step, comp, dates + d] = zero
            for c in range(3):
                acc[step, c, d] = zero
        tot[step] = zero
        return carry

    lax.fori_loop(0, ITERS, clear_state, 0)

    def clear_last(o, carry):
        for c in range(3):
            for d in range(band):
                gam[o, c, pl.ds((pad + dates - band + d) * rows, rows)] = zero
        return carry

    lax.fori_loop(0, band, clear_last, 0)

    pl.semaphore_wait(barrier, nd - 1 + has_up.astype(jnp.int32) + has_down.astype(jnp.int32))
    for k in range(1, nd):
        give(k, 0).start()
    fetch_own.wait()

    start = FIRST if nd == 2 else parts

    def send(n, carry):
        @pl.when(n < start)
        def _():
            take(0, n)

        @pl.when(n == 0)
        def _():
            fetch.wait()
            lax.fori_loop(0, nd, pack_rim, 0)
            start_halos(own, parts)
            for k in range(1, nd):
                give_rim(k).start()

        @pl.when(n > 0)
        def _():
            for k in range(1, nd):
                give(k, n).start()

        return carry

    lax.fori_loop(0, parts, send, 0)

    inner = lax.broadcasted_iota(jnp.int32, (dates, dates), 0)
    outer = lax.broadcasted_iota(jnp.int32, (dates, dates), 1)
    order = (inner == jnp.where(turn, dates - 1 - outer, outer)).astype(jnp.float32).astype(jnp.bfloat16)
    fetch_net.wait()
    mask = jnp.transpose(net_ref[...].astype(jnp.float32), (1, 0)).astype(jnp.bfloat16)
    mask = jnp.dot(order, mask, preferred_element_type=jnp.float32)

    def spread(o, carry):
        column = lax.broadcasted_iota(jnp.int32, (dates, band), 1) == o
        column = jnp.sum(jnp.where(column, mask, 0.0), axis=1, keepdims=True)
        used_at[o, pl.ds(0, pad)] = jnp.zeros((pad, width), jnp.float32)
        used_at[o, pl.ds(pad, dates)] = jnp.broadcast_to(column, (dates, width))
        return carry

    lax.fori_loop(0, band, spread, 0)
    def forward_rim(k):
        give_rim(k).wait_recv()
        start_halos(slab_of(k), parts)

    def forward(k, n):
        give(k, n).wait_recv()
        take(k, n)

    if nd != 2:
        for k in range(1, nd):
            forward_rim(k)
            for n in range(parts):
                forward(k, n)

    lane = lax.broadcasted_iota(jnp.int32, (SUB, width), 1)

    def open_slab(slab):
        def part(comp, carry):
            here = [main[comp, r, aligned(rims + slab * SUB)] for r in range(tall)]
            last = [main[comp, r, pl.ds(work + SUB, SUB)] for r in range(tall)]
            ends = lane >= slot * (groups - 1)
            earlier = [pltpu.roll(jnp.where(ends, b, a), slot % width, 1) for a, b in zip(here, last)]
            for r in range(tall):
                main[comp, r, pl.ds(work, SUB)] = earlier[r]
                main[comp, r, pl.ds(work + SUB, SUB)] = here[r]
            return carry

        lax.fori_loop(0, 2, part, 0)

    def pair_rows(o, base):
        part_re, part_im = [], []
        here, ahead = aligned(base), pl.ds(base - o, SUB)
        for r in range(tall):
            a_re, a_im = main[0, r, ahead], main[1, r, ahead]
            b_re, b_im = main[0, r, here], main[1, r, here]
            part_re.append(a_re * b_re + a_im * b_im)
            part_im.append(a_im * b_re - a_re * b_im)
        return halves(row_sums(part_re) + row_sums(part_im))

    each = 2 * rows * SUB

    def rim_sums():
        base = work + SUB
        rim_maps[pl.ds(0, each // 2)] = square_rows(base)

        def offset(o, carry):
            begin = pl.multiple_of(each // 2 + (o - 1) * each, each // 2)
            rim_maps[pl.ds(begin, each)] = pair_rows(o, base)
            return carry

        lax.fori_loop(1, band + 1, offset, 0)

    def square_rows(base):
        squares = []
        for r in range(tall):
            re, im = main[0, r, aligned(base)], main[1, r, aligned(base)]
            squares.append(re * re + im * im)
        return halves(row_sums(squares))

    def tile_sums(t):
        g = lax.rem(t, groups)
        base = SUB + t * SUB
        to = pad + t * SUB
        here = aligned(to)

        def column_sums(rows_of, begin):
            rim = rim_maps[pl.ds(begin, rows_of.shape[0])]
            table = jnp.concatenate([box[...], edges[g]], axis=0)
            return jnp.dot(jnp.concatenate([rows_of, rim], axis=1), table, preferred_element_type=jnp.float32)

        power = lax.rsqrt(column_sums(square_rows(base), 0) + EPS)
        for k in range(rows):
            root[k, here] = power[k * SUB : (k + 1) * SUB]
        for i in range(0, band, STRIDE):
            begin = each // 2 + i * each
            sums = column_sums(jnp.concatenate([pair_rows(i + s + 1, base) for s in range(STRIDE)], axis=0), begin)
            for s in range(STRIDE):
                o = i + s + 1
                used = used_at[o - 1, pl.ds(jnp.where(turn, to, to - o), SUB)]
                for k in range(rows):
                    weight = root[k, here] * root[k, pl.ds(to - o, SUB)] * used
                    at = pl.ds((to - o) * rows + k, SUB, stride=rows)
                    c_re = sums[s * each + k * SUB : s * each + (k + 1) * SUB] * weight
                    c_im = sums[s * each + (rows + k) * SUB : s * each + (rows + k + 1) * SUB] * weight
                    gam[o - 1, 0, at] = c_re
                    gam[o - 1, 1, at] = c_re + c_im
                    gam[o - 1, 2, at] = c_im - c_re

    def at_date(d):
        return pl.ds(pl.multiple_of((pad + d) * rows, rows), rows)

    def first(j):
        back_re = [acc[0, 0, i] for i in range(band)]
        back_sum = [acc[0, 1, i] for i in range(band)]
        total = tot[0]
        for i in range(SUB):
            d = j * SUB + i
            y_re = back_re[i] + 1.0
            y_im = back_re[i] - back_sum[i]
            ahead_re = ahead_sum = None
            for o in range(1, band + 1):
                c_re = gam[o - 1, 0, at_date(d)]
                c_sum = gam[o - 1, 1, at_date(d)]
                ahead_re = c_re if ahead_re is None else ahead_re + c_re
                ahead_sum = c_sum if ahead_sum is None else ahead_sum + c_sum
                if o == band:
                    back_re.append(c_re)
                    back_sum.append(c_sum)
                else:
                    back_re[i + o] = back_re[i + o] + c_re
                    back_sum[i + o] = back_sum[i + o] + c_sum
            y_re = y_re + ahead_re
            y_im = y_im + (ahead_sum - ahead_re)
            vec[0, 0, d] = y_re
            vec[0, 1, d] = y_im
            total = total + (y_re * y_re + y_im * y_im)
        for i in range(band):
            acc[0, 0, i] = back_re[SUB + i]
            acc[0, 1, i] = back_sum[SUB + i]
        tot[0] = total

    def later(step, j):
        acc_a, acc_b, acc_c = [[acc[step, c, i] for i in range(band)] for c in range(3)]
        base = j * SUB
        v_re = [vec[step - 1, 0, base + i] for i in range(band)]
        v_im = [vec[step - 1, 1, base + i] for i in range(band)]
        v_sum = [a + b for a, b in zip(v_re, v_im)]
        total = tot[step]
        for i in range(SUB):
            d = base + i
            v_re.append(vec[step - 1, 0, d + band])
            v_im.append(vec[step - 1, 1, d + band])
            v_sum.append(v_re[-1] + v_im[-1])
            y_a, y_b, y_c = acc_a[i], -acc_b[i], -acc_c[i]
            for o in range(1, band + 1):
                c_re = gam[o - 1, 0, at_date(d)]
                c_sum = gam[o - 1, 1, at_date(d)]
                c_dif = gam[o - 1, 2, at_date(d)]
                y_a = y_a + c_re * v_sum[i + o]
                y_b = y_b + c_dif * v_re[i + o]
                y_c = y_c + c_sum * v_im[i + o]
                back_a = c_re * v_sum[i]
                back_b = c_sum * v_re[i]
                back_c = c_dif * v_im[i]
                if o == band:
                    acc_a.append(back_a)
                    acc_b.append(back_b)
                    acc_c.append(back_c)
                else:
                    acc_a[i + o] = acc_a[i + o] + back_a
                    acc_b[i + o] = acc_b[i + o] + back_b
                    acc_c[i + o] = acc_c[i + o] + back_c
            y_re = v_re[i] + (y_a - y_c)
            y_im = v_im[i] + (y_a + y_b)
            vec[step, 0, d] = y_re
            vec[step, 1, d] = y_im
            total = total + (y_re * y_re + y_im * y_im)
        for i in range(band):
            acc[step, 0, i] = acc_a[SUB + i]
            acc[step, 1, i] = acc_b[SUB + i]
            acc[step, 2, i] = acc_c[SUB + i]
        tot[step] = total

    def advance(t, carry):
        if nd == 2:

            @pl.when(t < parts - start)
            def _():
                take(0, t + start)

            @pl.when(t == groups - EDGES)
            def _():
                forward_rim(1)

            past = t - groups + AHEAD

            @pl.when((past >= 0) & (lax.rem(past, span) == 0) & (past < groups))
            def _():
                forward(1, lax.div(past, span))

        @pl.when(t < tiles)
        def _():
            slab, g = lax.div(t, groups), lax.rem(t, groups)

            @pl.when(g == 0)
            def _():
                await_halos(slab, parts)
                open_slab(slab)
                rim_sums()

            @pl.when(lax.rem(g, span) == 0)
            def _():
                await_halos(slab, lax.div(g, span))

            tile_sums(t)

        @pl.when((t >= 1) & (t <= tiles))
        def _():
            first(t - 1)

        def level(step, carry):
            later(step, t - 1 - step)
            return carry

        lax.fori_loop(jnp.maximum(1, t - tiles), jnp.minimum(t, ITERS), level, 0)
        return carry

    lax.fori_loop(0, tiles + ITERS, advance, 0)

    def sent(n, carry):
        for k in range(1, nd):
            give(k, n).wait_send()
        for s in range(nd):
            await_sent(s, n)
        return carry

    lax.fori_loop(0, parts, sent, 0)
    for k in range(1, nd):
        give_rim(k).wait_send()
    for s in range(nd):
        await_sent(s, parts)


def scale_kernel(nd, vec, tot, out_ref):
    dates = out_ref.shape[1]
    scale = None
    for step in range(ITERS):
        mean = tot[step] / dates
        if scale is None:
            scale = lax.rsqrt(mean + EPS)
        else:
            scale = scale * lax.rsqrt(scale * scale * mean + EPS)
    turn = 2 * lax.axis_index("date") >= nd

    def block(b, carry):
        for j in range(SUB):
            d = b * SUB + j
            at = jnp.where(turn, dates - 1 - d, d)
            for comp in range(2):
                out_ref[comp, at] = vec[ITERS - 1, comp, d] * scale
        return carry

    lax.fori_loop(0, dates // SUB, block, 0)


def odd(count):
    return count + 1 - count % 2


def on_device(nd, nr, slc, network):
    _, local, rows, cols = slc.shape
    width = cols // nd
    dates, band = network.shape
    tall = rows + 2 * LOOK
    maps = (2 * band + 1) * rows * SUB
    parts = local // PIECE if local % PIECE == 0 else 1
    whole = pl.BlockSpec(memory_space=pltpu.VMEM)
    away = pl.BlockSpec(memory_space=pltpu.HBM)
    f32, bf16 = jnp.float32, jnp.bfloat16
    sems = pltpu.SemaphoreType.DMA((nd, parts + 1))
    vec, tot = pl.pallas_call(
        functools.partial(main_kernel, nd, nr),
        out_shape=[
            pltpu.VMEM((ITERS, 2, dates + band, rows, width), f32),
            pltpu.VMEM((ITERS, rows, width), f32),
        ],
        in_specs=[away, away],
        out_specs=[whole, whole],
        scratch_shapes=[
            pltpu.VMEM((band, dates), network.dtype),
            pltpu.VMEM((2, local, rows, cols), f32),
            pltpu.VMEM((nd, 2, local, rows, width), f32),
            pltpu.VMEM((2, tall, odd(dates // SUB + 2 * nd + 2) * SUB, width), f32),
            pltpu.VMEM((maps, 2 * width), bf16),
            pltpu.VMEM((2 * width, width), bf16),
            pltpu.VMEM((local // SUB, 2 * width, width), bf16),
            pltpu.VMEM((rows, odd((2 * band + dates) // SUB) * SUB, width), f32),
            pltpu.VMEM((band, odd((2 * band + dates) // SUB) * SUB, width), f32),
            pltpu.VMEM((band, 3, odd(2 * band + dates) * rows, width), f32),
            pltpu.VMEM((ITERS, 3, band, rows, width), f32),
            pltpu.SemaphoreType.DMA((3,)),
        ]
        + [sems] * 6,
        compiler_params=pltpu.CompilerParams(
            collective_id=0, has_side_effects=True, vmem_limit_bytes=40 * 1024 * 1024
        ),
        name="link",
    )(pltpu.with_memory_space_constraint(slc, pltpu.HBM), pltpu.with_memory_space_constraint(network.T, pltpu.HBM))
    vec = pltpu.with_memory_space_constraint(vec, pltpu.VMEM)
    tot = pltpu.with_memory_space_constraint(tot, pltpu.VMEM)
    return pl.pallas_call(
        functools.partial(scale_kernel, nd),
        out_shape=jax.ShapeDtypeStruct((2, dates, rows, width), f32),
        in_specs=[whole, whole],
        out_specs=whole,
        compiler_params=pltpu.CompilerParams(vmem_limit_bytes=8 * 1024 * 1024),
        name="scale",
    )(vec, tot)


def solution(mesh):
    return jax.shard_map(
        functools.partial(on_device, mesh.shape["date"], mesh.shape["row"]),
        mesh=mesh,
        in_specs=(P(None, "date", "row", None), P()),
        out_specs=P(None, None, "row", "date"),
        check_vma=False,
    )
```

```python
import functools

import jax
import jax.numpy as jnp
from jax import lax
from jax.experimental import pallas as pl
from jax.experimental.pallas import tpu as pltpu
from jax.sharding import PartitionSpec as P

LOOK = 5
ITERS = 5
SUB = 8
PIECE = 8
AHEAD = 3
FIRST = 3
EDGES = 4
STRIDE = 2
EPS = 1e-06
MESH = pl.DeviceIdType.MESH


def row_sums(cells):
    span = 2 * LOOK + 1
    count = len(cells) - span + 1
    head = functools.reduce(jnp.add, cells[count - 1 : span])
    heads = [head]
    for k in range(count - 2, -1, -1):
        heads.append(heads[-1] + cells[k])
    heads = heads[::-1]
    sums = [heads[0]]
    tail = None
    for k in range(1, count):
        cell = cells[span + k - 1]
        tail = cell if tail is None else tail + cell
        sums.append(heads[k] + tail)
    return sums


def halves(sums):
    stacked = jnp.concatenate(sums, axis=0)
    high = stacked.astype(jnp.bfloat16)
    low = (stacked - high.astype(jnp.float32)).astype(jnp.bfloat16)
    return jnp.concatenate([high, low], axis=1)


def main_kernel(
    nd, nr, x_hbm, net_hbm, vec, tot,
    net_ref, x_ref, stack, main, held, rim_maps, box, edges, root, used_at, gam, acc, load_sem,
    give_send, give_recv, up_send, up_recv, down_send, down_recv,
):
    _, local, rows, _ = x_ref.shape
    width = main.shape[3]
    band, dates = net_ref.shape
    groups = local // SUB
    thin = nd == 2
    comps = 1 if thin else 2
    slot = width // groups // (3 - comps)
    tiles = dates // SUB
    tall = rows + 2 * LOOK
    work = SUB + dates
    rims = work + 2 * SUB
    pad = 2 * band
    parts = give_send.shape[1] - 1
    piece = local // parts
    span = piece // SUB
    me = lax.axis_index("date")
    row = lax.axis_index("row")
    has_up = row > 0
    has_down = row < nr - 1
    up = jnp.maximum(row - 1, 0)
    down = jnp.minimum(row + 1, nr - 1)

    def mirrored(device):
        return 2 * device >= nd

    def place(source, device):
        return jnp.where(mirrored(device), nd - 1 - source, source)

    own = place(me, me)
    turn = mirrored(me)
    barrier = pltpu.get_barrier_semaphore()
    for k in range(1, nd):
        pl.semaphore_signal(barrier, 1, device_id=(lax.rem(me + k, nd), row), device_id_type=MESH)

    @pl.when(has_up)
    def _():
        pl.semaphore_signal(barrier, 1, device_id=(me, up), device_id_type=MESH)

    @pl.when(has_down)
    def _():
        pl.semaphore_signal(barrier, 1, device_id=(me, down), device_id_type=MESH)

    def aligned(start, size=SUB):
        return pl.ds(pl.multiple_of(start, SUB), size)

    def columns(device):
        return pl.ds(pl.multiple_of(device * width, width), width)

    fetch_own = pltpu.make_async_copy(x_hbm.at[:, :, :, columns(me)], stack.at[0], load_sem.at[0])
    fetch_own.start()
    fetch = pltpu.make_async_copy(x_hbm, x_ref, load_sem.at[1])
    fetch.start()
    fetch_net = pltpu.make_async_copy(net_hbm, net_ref, load_sem.at[2])
    fetch_net.start()

    def give(k, n):
        there = lax.rem(me + k, nd)
        near = pl.ds(jnp.where(mirrored(there), local - (n + 1) * piece, n * piece), piece)
        return pltpu.make_async_remote_copy(
            src_ref=x_hbm.at[:, near, :, columns(there)],
            dst_ref=stack.at[k, :, near],
            send_sem=give_send.at[k, n],
            recv_sem=give_recv.at[k, n],
            device_id=(there, row),
            device_id_type=MESH,
        )

    def give_rim(k):
        there = lax.rem(me + k, nd)
        inner = pl.ds(LOOK, rows)
        return pltpu.make_async_remote_copy(
            src_ref=main.at[pl.ds(0, comps), inner, pl.ds(rims + (nd + k - 1) * SUB, SUB)],
            dst_ref=main.at[pl.ds(0, comps), inner, aligned(rims + place(me, there) * SUB)],
            send_sem=give_send.at[k, parts],
            recv_sem=give_recv.at[k, parts],
            device_id=(there, row),
            device_id_type=MESH,
        )

    def halo(slab, n, to_up, size):
        both = pl.ds(0, comps if n is parts else 2)
        near = aligned(rims + slab * SUB if n is parts else SUB + slab * local + n * piece, size)
        return pltpu.make_async_remote_copy(
            src_ref=main.at[both, pl.ds(LOOK if to_up else rows, LOOK), near],
            dst_ref=main.at[both, pl.ds(LOOK + rows if to_up else 0, LOOK), near],
            send_sem=(up_send if to_up else down_send).at[slab, n],
            recv_sem=(up_recv if to_up else down_recv).at[slab, n],
            device_id=(me, up if to_up else down),
            device_id_type=MESH,
        )

    def both_ways(slab, n, act):
        size = SUB if n is parts else piece

        @pl.when(has_up)
        def _():
            act(halo(slab, n, True, size), halo(slab, n, False, size))

        @pl.when(has_down)
        def _():
            act(halo(slab, n, False, size), halo(slab, n, True, size))

    def start_halos(slab, n):
        both_ways(slab, n, lambda there, back: there.start())

    def await_halos(slab, n):
        both_ways(slab, n, lambda there, back: back.wait_recv())

    def await_sent(slab, n):
        both_ways(slab, n, lambda there, back: there.wait_send())

    def slab_of(k):
        return place(lax.rem(me + nd - k, nd), me)

    def turned(cells):
        return jnp.transpose(jnp.stack(cells), (1, 0, 2))

    def take(k, n):
        slab = slab_of(k)
        for s in range(span):
            for comp in range(2):
                cells = []
                for j in range(SUB):
                    d = n * piece + s * SUB + j
                    cells.append(stack[k, comp, jnp.where(turn, local - 1 - d, d)])
                at = SUB + slab * local + n * piece + s * SUB
                main[comp, pl.ds(LOOK, rows), aligned(at)] = turned(cells)
        start_halos(slab, n)

    zero = jnp.zeros((rows, width), jnp.float32)
    blank = jnp.zeros((SUB, width), jnp.float32)
    lane = lax.broadcasted_iota(jnp.int32, (rows, width), 1)

    def pack_rim(k, carry):
        device = lax.rem(me + k, nd)
        back = mirrored(device)
        at = rims + jnp.where(k == 0, own, nd + k - 1) * SUB
        shift = LOOK
        if thin:
            sides = [(1 - device, 0, LOOK)]
            shift = jnp.where(device > 0, LOOK, 0)
        else:
            sides = [(jnp.maximum(device - 1, 0), 0, LOOK), (jnp.minimum(device + 1, nd - 1), LOOK, 2 * LOOK)]

        def group(g, cells):
            cells = list(cells)
            for comp in range(2):
                begin = slot * g + (comp * (width // 2) if thin else 0)
                for j in range(SUB):
                    d = g * SUB + j
                    d = jnp.where(back, local - 1 - d, d)
                    i = j if thin else comp * SUB + j
                    for block, low, high in sides:
                        moved = pltpu.roll(x_ref[comp, d, :, columns(block)], begin + shift, 1)
                        cells[i] = jnp.where((lane >= begin + low) & (lane < begin + high), moved, cells[i])
            return tuple(cells)

        cells = lax.fori_loop(0, groups, group, tuple(zero for _ in range(comps * SUB)), unroll=4)
        for comp in range(comps):
            main[comp, pl.ds(LOOK, rows), aligned(at)] = turned(cells[comp * SUB : (comp + 1) * SUB])
        return carry

    def clear_rows(begin):
        def clear(i, carry):
            main[lax.rem(i, 2), begin + lax.div(i, 2), pl.ds(0, rims + nd * SUB)] = jnp.zeros((rims + nd * SUB, width), jnp.float32)
            return carry

        lax.fori_loop(0, 2 * LOOK, clear, 0)

    @pl.when(jnp.logical_not(has_up))
    def _():
        clear_rows(0)

    @pl.when(jnp.logical_not(has_down))
    def _():
        clear_rows(LOOK + rows)

    def clear_front(r, carry):
        for comp in range(2):
            main[comp, r, pl.ds(0, SUB)] = blank
            main[comp, r, pl.ds(work + SUB, SUB)] = blank
        return carry

    lax.fori_loop(0, tall, clear_front, 0)
    inner = lax.broadcasted_iota(jnp.int32, (width, width), 0)
    outer = lax.broadcasted_iota(jnp.int32, (width, width), 1)
    near = (jnp.abs(inner - outer) <= LOOK).astype(jnp.float32).astype(jnp.bfloat16)
    box[pl.ds(0, width)] = near
    box[pl.ds(width, width)] = near

    def edge_table(g, carry):
        cell = inner - slot * g
        left = (cell >= 0) & (cell < LOOK) & (outer <= cell) & (me > 0)
        if not thin:
            cell = cell - LOOK
        right = (cell >= 0) & (cell < LOOK) & (outer >= width + cell - LOOK) & (me < nd - 1)
        edge = (left | right).astype(jnp.float32).astype(jnp.bfloat16)
        edges[g, pl.ds(0, width)] = edge
        edges[g, pl.ds(width, width)] = edge
        return carry

    lax.fori_loop(0, groups, edge_table, 0)
    for k in range(rows):
        root[k, pl.ds(0, pad)] = jnp.zeros((pad, width), jnp.float32)

    def clear_state(step, carry):
        for d in range(band):
            for comp in range(2):
                vec[step, comp, dates + d] = zero
            for c in range(3):
                acc[step, c, d] = zero
        tot[step] = zero
        return carry

    lax.fori_loop(0, ITERS, clear_state, 0)

    def clear_last(o, carry):
        for c in range(3):
            for d in range(band):
                gam[o, c, pl.ds((pad + dates - band + d) * rows, rows)] = zero
        return carry

    lax.fori_loop(0, band, clear_last, 0)

    pl.semaphore_wait(barrier, nd - 1 + has_up.astype(jnp.int32) + has_down.astype(jnp.int32))
    fetch_own.wait()

    start = FIRST if nd == 2 else parts

    def send(n, carry):
        @pl.when(n < start)
        def _():
            take(0, n)

        @pl.when(n == 0)
        def _():
            for k in range(1, nd):
                give(k, 0).start()
            fetch.wait()
            lax.fori_loop(0, nd, pack_rim, 0)
            start_halos(own, parts)
            for k in range(1, nd):
                give_rim(k).start()

        @pl.when(n > 0)
        def _():
            for k in range(1, nd):
                give(k, n).start()

        return carry

    lax.fori_loop(0, parts, send, 0)

    inner = lax.broadcasted_iota(jnp.int32, (dates, dates), 0)
    outer = lax.broadcasted_iota(jnp.int32, (dates, dates), 1)
    order = (inner == jnp.where(turn, dates - 1 - outer, outer)).astype(jnp.float32).astype(jnp.bfloat16)
    fetch_net.wait()
    mask = jnp.transpose(net_ref[...].astype(jnp.float32), (1, 0)).astype(jnp.bfloat16)
    mask = jnp.dot(order, mask, preferred_element_type=jnp.float32)

    def spread(o, carry):
        column = lax.broadcasted_iota(jnp.int32, (dates, band), 1) == o
        column = jnp.sum(jnp.where(column, mask, 0.0), axis=1, keepdims=True)
        used_at[o, pl.ds(0, pad)] = jnp.zeros((pad, width), jnp.float32)
        used_at[o, pl.ds(pad, dates)] = jnp.broadcast_to(column, (dates, width))
        return carry

    lax.fori_loop(0, band, spread, 0)
    def forward_rim(k):
        give_rim(k).wait_recv()
        start_halos(slab_of(k), parts)

    def forward(k, n):
        give(k, n).wait_recv()
        take(k, n)

    if nd != 2:
        for k in range(1, nd):
            forward_rim(k)
            for n in range(parts):
                forward(k, n)

    lane = lax.broadcasted_iota(jnp.int32, (SUB, width), 1)

    def open_slab(slab):
        def part(comp, carry):
            from_comp = 0 if thin else comp
            last_comp = 1 - comp if thin else comp
            here = [main[from_comp, r, aligned(rims + slab * SUB)] for r in range(tall)]
            last = [main[last_comp, r, pl.ds(work + SUB, SUB)] for r in range(tall)]
            if thin:
                here = [pltpu.roll(cell, comp * (width // 2), 1) for cell in here]
            ends = lane >= width - slot
            earlier = [pltpu.roll(jnp.where(ends, b, a), slot % width, 1) for a, b in zip(here, last)]
            for r in range(tall):
                main[comp, r, pl.ds(work, SUB)] = earlier[r]
                held[comp, r] = here[r]
            return carry

        lax.fori_loop(0, 2, part, 0)

        def keep(r, carry):
            for comp in range(2):
                main[comp, r, pl.ds(work + SUB, SUB)] = held[comp, r]
            return carry

        lax.fori_loop(0, tall, keep, 0)

    def pair_rows(o, base):
        part_re, part_im = [], []
        here, ahead = aligned(base), pl.ds(base - o, SUB)
        for r in range(tall):
            a_re, a_im = main[0, r, ahead], main[1, r, ahead]
            b_re, b_im = main[0, r, here], main[1, r, here]
            part_re.append(a_re * b_re + a_im * b_im)
            part_im.append(a_im * b_re - a_re * b_im)
        return halves(row_sums(part_re) + row_sums(part_im))

    each = 2 * rows * SUB

    def rim_sums():
        base = work + SUB
        rim_maps[pl.ds(0, each // 2)] = square_rows(base)

        def offset(o, carry):
            begin = pl.multiple_of(each // 2 + (o - 1) * each, each // 2)
            rim_maps[pl.ds(begin, each)] = pair_rows(o, base)
            return carry

        lax.fori_loop(1, band + 1, offset, 0)

    def square_rows(base):
        squares = []
        for r in range(tall):
            re, im = main[0, r, aligned(base)], main[1, r, aligned(base)]
            squares.append(re * re + im * im)
        return halves(row_sums(squares))

    def tile_sums(t):
        g = lax.rem(t, groups)
        base = SUB + t * SUB
        to = pad + t * SUB
        here = aligned(to)

        def column_sums(rows_of, begin):
            rim = rim_maps[pl.ds(begin, rows_of.shape[0])]
            table = jnp.concatenate([box[...], edges[g]], axis=0)
            return jnp.dot(jnp.concatenate([rows_of, rim], axis=1), table, preferred_element_type=jnp.float32)

        power = lax.rsqrt(column_sums(square_rows(base), 0) + EPS)
        for k in range(rows):
            root[k, here] = power[k * SUB : (k + 1) * SUB]
        for i in range(0, band, STRIDE):
            begin = each // 2 + i * each
            sums = column_sums(jnp.concatenate([pair_rows(i + s + 1, base) for s in range(STRIDE)], axis=0), begin)
            for s in range(STRIDE):
                o = i + s + 1
                used = used_at[o - 1, pl.ds(jnp.where(turn, to, to - o), SUB)]
                for k in range(rows):
                    weight = root[k, here] * root[k, pl.ds(to - o, SUB)] * used
                    at = pl.ds((to - o) * rows + k, SUB, stride=rows)
                    c_re = sums[s * each + k * SUB : s * each + (k + 1) * SUB] * weight
                    c_im = sums[s * each + (rows + k) * SUB : s * each + (rows + k + 1) * SUB] * weight
                    gam[o - 1, 0, at] = c_re
                    gam[o - 1, 1, at] = c_re + c_im
                    gam[o - 1, 2, at] = c_im - c_re

    def at_date(d):
        return pl.ds(pl.multiple_of((pad + d) * rows, rows), rows)

    def first(j):
        back_re = [acc[0, 0, i] for i in range(band)]
        back_sum = [acc[0, 1, i] for i in range(band)]
        total = tot[0]
        for i in range(SUB):
            d = j * SUB + i
            y_re = back_re[i] + 1.0
            y_im = back_re[i] - back_sum[i]
            ahead_re = ahead_sum = None
            for o in range(1, band + 1):
                c_re = gam[o - 1, 0, at_date(d)]
                c_sum = gam[o - 1, 1, at_date(d)]
                ahead_re = c_re if ahead_re is None else ahead_re + c_re
                ahead_sum = c_sum if ahead_sum is None else ahead_sum + c_sum
                if o == band:
                    back_re.append(c_re)
                    back_sum.append(c_sum)
                else:
                    back_re[i + o] = back_re[i + o] + c_re
                    back_sum[i + o] = back_sum[i + o] + c_sum
            y_re = y_re + ahead_re
            y_im = y_im + (ahead_sum - ahead_re)
            vec[0, 0, d] = y_re
            vec[0, 1, d] = y_im
            total = total + (y_re * y_re + y_im * y_im)
        for i in range(band):
            acc[0, 0, i] = back_re[SUB + i]
            acc[0, 1, i] = back_sum[SUB + i]
        tot[0] = total

    def later(step, j):
        acc_a, acc_b, acc_c = [[acc[step, c, i] for i in range(band)] for c in range(3)]
        base = j * SUB
        v_re = [vec[step - 1, 0, base + i] for i in range(band)]
        v_im = [vec[step - 1, 1, base + i] for i in range(band)]
        v_sum = [a + b for a, b in zip(v_re, v_im)]
        total = tot[step]
        for i in range(SUB):
            d = base + i
            v_re.append(vec[step - 1, 0, d + band])
            v_im.append(vec[step - 1, 1, d + band])
            v_sum.append(v_re[-1] + v_im[-1])
            y_a, y_b, y_c = acc_a[i], -acc_b[i], -acc_c[i]
            for o in range(1, band + 1):
                c_re = gam[o - 1, 0, at_date(d)]
                c_sum = gam[o - 1, 1, at_date(d)]
                c_dif = gam[o - 1, 2, at_date(d)]
                y_a = y_a + c_re * v_sum[i + o]
                y_b = y_b + c_dif * v_re[i + o]
                y_c = y_c + c_sum * v_im[i + o]
                back_a = c_re * v_sum[i]
                back_b = c_sum * v_re[i]
                back_c = c_dif * v_im[i]
                if o == band:
                    acc_a.append(back_a)
                    acc_b.append(back_b)
                    acc_c.append(back_c)
                else:
                    acc_a[i + o] = acc_a[i + o] + back_a
                    acc_b[i + o] = acc_b[i + o] + back_b
                    acc_c[i + o] = acc_c[i + o] + back_c
            y_re = v_re[i] + (y_a - y_c)
            y_im = v_im[i] + (y_a + y_b)
            vec[step, 0, d] = y_re
            vec[step, 1, d] = y_im
            total = total + (y_re * y_re + y_im * y_im)
        for i in range(band):
            acc[step, 0, i] = acc_a[SUB + i]
            acc[step, 1, i] = acc_b[SUB + i]
            acc[step, 2, i] = acc_c[SUB + i]
        tot[step] = total

    def advance(t, carry):
        if nd == 2:

            @pl.when(t < parts - start)
            def _():
                take(0, t + start)

            @pl.when(t == groups - EDGES)
            def _():
                forward_rim(1)

            past = t - groups + AHEAD

            @pl.when((past >= 0) & (lax.rem(past, span) == 0) & (past < groups))
            def _():
                forward(1, lax.div(past, span))

        @pl.when(t < tiles)
        def _():
            slab, g = lax.div(t, groups), lax.rem(t, groups)

            @pl.when(g == 0)
            def _():
                await_halos(slab, parts)
                open_slab(slab)
                rim_sums()

            @pl.when(lax.rem(g, span) == 0)
            def _():
                await_halos(slab, lax.div(g, span))

            tile_sums(t)

        @pl.when((t >= 1) & (t <= tiles))
        def _():
            first(t - 1)

        def level(step, carry):
            later(step, t - 1 - step)
            return carry

        lax.fori_loop(jnp.maximum(1, t - tiles), jnp.minimum(t, ITERS), level, 0)
        return carry

    lax.fori_loop(0, tiles + ITERS, advance, 0)

    def sent(n, carry):
        for k in range(1, nd):
            give(k, n).wait_send()
        for s in range(nd):
            await_sent(s, n)
        return carry

    lax.fori_loop(0, parts, sent, 0)
    for k in range(1, nd):
        give_rim(k).wait_send()
    for s in range(nd):
        await_sent(s, parts)


def scale_kernel(nd, vec, tot, out_ref):
    dates = out_ref.shape[1]
    scale = None
    for step in range(ITERS):
        mean = tot[step] / dates
        if scale is None:
            scale = lax.rsqrt(mean + EPS)
        else:
            scale = scale * lax.rsqrt(scale * scale * mean + EPS)
    turn = 2 * lax.axis_index("date") >= nd

    def block(b, carry):
        for j in range(SUB):
            d = b * SUB + j
            at = jnp.where(turn, dates - 1 - d, d)
            for comp in range(2):
                out_ref[comp, at] = vec[ITERS - 1, comp, d] * scale
        return carry

    lax.fori_loop(0, dates // SUB, block, 0)


def odd(count):
    return count + 1 - count % 2


def on_device(nd, nr, slc, network):
    _, local, rows, cols = slc.shape
    width = cols // nd
    dates, band = network.shape
    tall = rows + 2 * LOOK
    maps = (2 * band + 1) * rows * SUB
    parts = local // PIECE if local % PIECE == 0 else 1
    whole = pl.BlockSpec(memory_space=pltpu.VMEM)
    away = pl.BlockSpec(memory_space=pltpu.HBM)
    f32, bf16 = jnp.float32, jnp.bfloat16
    sems = pltpu.SemaphoreType.DMA((nd, parts + 1))
    vec, tot = pl.pallas_call(
        functools.partial(main_kernel, nd, nr),
        out_shape=[
            pltpu.VMEM((ITERS, 2, dates + band, rows, width), f32),
            pltpu.VMEM((ITERS, rows, width), f32),
        ],
        in_specs=[away, away],
        out_specs=[whole, whole],
        scratch_shapes=[
            pltpu.VMEM((band, dates), network.dtype),
            pltpu.VMEM((2, local, rows, cols), f32),
            pltpu.VMEM((nd, 2, local, rows, width), f32),
            pltpu.VMEM((2, tall, odd(dates // SUB + 2 * nd + 2) * SUB, width), f32),
            pltpu.VMEM((2, tall, SUB, width), f32),
            pltpu.VMEM((maps, 2 * width), bf16),
            pltpu.VMEM((2 * width, width), bf16),
            pltpu.VMEM((local // SUB, 2 * width, width), bf16),
            pltpu.VMEM((rows, odd((2 * band + dates) // SUB) * SUB, width), f32),
            pltpu.VMEM((band, odd((2 * band + dates) // SUB) * SUB, width), f32),
            pltpu.VMEM((band, 3, odd(2 * band + dates) * rows, width), f32),
            pltpu.VMEM((ITERS, 3, band, rows, width), f32),
            pltpu.SemaphoreType.DMA((3,)),
        ]
        + [sems] * 6,
        compiler_params=pltpu.CompilerParams(
            collective_id=0, has_side_effects=True, vmem_limit_bytes=40 * 1024 * 1024
        ),
        name="link",
    )(pltpu.with_memory_space_constraint(slc, pltpu.HBM), pltpu.with_memory_space_constraint(network.T, pltpu.HBM))
    vec = pltpu.with_memory_space_constraint(vec, pltpu.VMEM)
    tot = pltpu.with_memory_space_constraint(tot, pltpu.VMEM)
    return pl.pallas_call(
        functools.partial(scale_kernel, nd),
        out_shape=jax.ShapeDtypeStruct((2, dates, rows, width), f32),
        in_specs=[whole, whole],
        out_specs=whole,
        compiler_params=pltpu.CompilerParams(vmem_limit_bytes=8 * 1024 * 1024),
        name="scale",
    )(vec, tot)


def solution(mesh):
    return jax.shard_map(
        functools.partial(on_device, mesh.shape["date"], mesh.shape["row"]),
        mesh=mesh,
        in_specs=(P(None, "date", "row", None), P()),
        out_specs=P(None, None, "row", "date"),
        check_vma=False,
    )
```

```python
import functools

import jax
import jax.numpy as jnp
from jax import lax
from jax.experimental import pallas as pl
from jax.experimental.pallas import tpu as pltpu
from jax.sharding import PartitionSpec as P

LOOK = 5
ITERS = 5
SUB = 8
PIECE = 8
AHEAD = 3
FIRST = 3
EDGES = 4
STRIDE = 2
STEPS = 2
EPS = 1e-06
MESH = pl.DeviceIdType.MESH


def row_sums(cells):
    span = 2 * LOOK + 1
    count = len(cells) - span + 1
    head = functools.reduce(jnp.add, cells[count - 1 : span])
    heads = [head]
    for k in range(count - 2, -1, -1):
        heads.append(heads[-1] + cells[k])
    heads = heads[::-1]
    sums = [heads[0]]
    tail = None
    for k in range(1, count):
        cell = cells[span + k - 1]
        tail = cell if tail is None else tail + cell
        sums.append(heads[k] + tail)
    return sums


def halves(sums):
    stacked = jnp.concatenate(sums, axis=0)
    high = stacked.astype(jnp.bfloat16)
    low = (stacked - high.astype(jnp.float32)).astype(jnp.bfloat16)
    return jnp.concatenate([high, low], axis=1)


def main_kernel(
    nd, nr, x_hbm, net_hbm, vec, tot,
    net_ref, x_ref, stack, main, held, rim_maps, box, edges, root, used_at, gam, acc, load_sem,
    give_send, give_recv, up_send, up_recv, down_send, down_recv,
):
    _, local, rows, _ = x_ref.shape
    width = main.shape[3]
    band, dates = net_ref.shape
    groups = local // SUB
    thin = nd == 2
    comps = 1 if thin else 2
    slot = width // groups // (3 - comps)
    tiles = dates // SUB
    tall = rows + 2 * LOOK
    work = SUB + dates
    rims = work + 2 * SUB
    pad = 2 * band
    parts = give_send.shape[1] - 1
    piece = local // parts
    span = piece // SUB
    me = lax.axis_index("date")
    row = lax.axis_index("row")
    has_up = row > 0
    has_down = row < nr - 1
    up = jnp.maximum(row - 1, 0)
    down = jnp.minimum(row + 1, nr - 1)

    def mirrored(device):
        return 2 * device >= nd

    def place(source, device):
        return jnp.where(mirrored(device), nd - 1 - source, source)

    own = place(me, me)
    turn = mirrored(me)
    barrier = pltpu.get_barrier_semaphore()
    for k in range(1, nd):
        pl.semaphore_signal(barrier, 1, device_id=(lax.rem(me + k, nd), row), device_id_type=MESH)

    @pl.when(has_up)
    def _():
        pl.semaphore_signal(barrier, 1, device_id=(me, up), device_id_type=MESH)

    @pl.when(has_down)
    def _():
        pl.semaphore_signal(barrier, 1, device_id=(me, down), device_id_type=MESH)

    def aligned(start, size=SUB):
        return pl.ds(pl.multiple_of(start, SUB), size)

    def columns(device):
        return pl.ds(pl.multiple_of(device * width, width), width)

    fetch_own = pltpu.make_async_copy(x_hbm.at[:, :, :, columns(me)], stack.at[0], load_sem.at[0])
    fetch_own.start()
    fetch = pltpu.make_async_copy(x_hbm, x_ref, load_sem.at[1])
    fetch.start()
    fetch_net = pltpu.make_async_copy(net_hbm, net_ref, load_sem.at[2])
    fetch_net.start()

    def give(k, n):
        there = lax.rem(me + k, nd)
        near = pl.ds(jnp.where(mirrored(there), local - (n + 1) * piece, n * piece), piece)
        return pltpu.make_async_remote_copy(
            src_ref=x_hbm.at[:, near, :, columns(there)],
            dst_ref=stack.at[k, :, near],
            send_sem=give_send.at[k, n],
            recv_sem=give_recv.at[k, n],
            device_id=(there, row),
            device_id_type=MESH,
        )

    def give_rim(k):
        there = lax.rem(me + k, nd)
        inner = pl.ds(LOOK, rows)
        return pltpu.make_async_remote_copy(
            src_ref=main.at[pl.ds(0, comps), inner, pl.ds(rims + (nd + k - 1) * SUB, SUB)],
            dst_ref=main.at[pl.ds(0, comps), inner, aligned(rims + place(me, there) * SUB)],
            send_sem=give_send.at[k, parts],
            recv_sem=give_recv.at[k, parts],
            device_id=(there, row),
            device_id_type=MESH,
        )

    def halo(slab, n, to_up, size):
        both = pl.ds(0, comps if n is parts else 2)
        near = aligned(rims + slab * SUB if n is parts else SUB + slab * local + n * piece, size)
        return pltpu.make_async_remote_copy(
            src_ref=main.at[both, pl.ds(LOOK if to_up else rows, LOOK), near],
            dst_ref=main.at[both, pl.ds(LOOK + rows if to_up else 0, LOOK), near],
            send_sem=(up_send if to_up else down_send).at[slab, n],
            recv_sem=(up_recv if to_up else down_recv).at[slab, n],
            device_id=(me, up if to_up else down),
            device_id_type=MESH,
        )

    def both_ways(slab, n, act):
        size = SUB if n is parts else piece

        @pl.when(has_up)
        def _():
            act(halo(slab, n, True, size), halo(slab, n, False, size))

        @pl.when(has_down)
        def _():
            act(halo(slab, n, False, size), halo(slab, n, True, size))

    def start_halos(slab, n):
        both_ways(slab, n, lambda there, back: there.start())

    def await_halos(slab, n):
        both_ways(slab, n, lambda there, back: back.wait_recv())

    def await_sent(slab, n):
        both_ways(slab, n, lambda there, back: there.wait_send())

    def slab_of(k):
        return place(lax.rem(me + nd - k, nd), me)

    def turned(cells):
        return jnp.transpose(jnp.stack(cells), (1, 0, 2))

    def take(k, n):
        slab = slab_of(k)
        for s in range(span):
            for comp in range(2):
                cells = []
                for j in range(SUB):
                    d = n * piece + s * SUB + j
                    cells.append(stack[k, comp, jnp.where(turn, local - 1 - d, d)])
                at = SUB + slab * local + n * piece + s * SUB
                main[comp, pl.ds(LOOK, rows), aligned(at)] = turned(cells)
        start_halos(slab, n)

    zero = jnp.zeros((rows, width), jnp.float32)
    blank = jnp.zeros((SUB, width), jnp.float32)
    lane = lax.broadcasted_iota(jnp.int32, (rows, width), 1)

    def pack_rim(k, carry):
        device = lax.rem(me + k, nd)
        back = mirrored(device)
        at = rims + jnp.where(k == 0, own, nd + k - 1) * SUB
        shift = LOOK
        if thin:
            sides = [(1 - device, 0, LOOK)]
            shift = jnp.where(device > 0, LOOK, 0)
        else:
            sides = [(jnp.maximum(device - 1, 0), 0, LOOK), (jnp.minimum(device + 1, nd - 1), LOOK, 2 * LOOK)]

        def group(g, cells):
            cells = list(cells)
            for comp in range(2):
                begin = slot * g + (comp * (width // 2) if thin else 0)
                for j in range(SUB):
                    d = g * SUB + j
                    d = jnp.where(back, local - 1 - d, d)
                    i = j if thin else comp * SUB + j
                    for block, low, high in sides:
                        moved = pltpu.roll(x_ref[comp, d, :, columns(block)], begin + shift, 1)
                        cells[i] = jnp.where((lane >= begin + low) & (lane < begin + high), moved, cells[i])
            return tuple(cells)

        cells = lax.fori_loop(0, groups, group, tuple(zero for _ in range(comps * SUB)), unroll=4)
        for comp in range(comps):
            main[comp, pl.ds(LOOK, rows), aligned(at)] = turned(cells[comp * SUB : (comp + 1) * SUB])
        return carry

    def clear_rows(begin):
        def clear(i, carry):
            main[lax.rem(i, 2), begin + lax.div(i, 2), pl.ds(0, rims + nd * SUB)] = jnp.zeros((rims + nd * SUB, width), jnp.float32)
            return carry

        lax.fori_loop(0, 2 * LOOK, clear, 0)

    @pl.when(jnp.logical_not(has_up))
    def _():
        clear_rows(0)

    @pl.when(jnp.logical_not(has_down))
    def _():
        clear_rows(LOOK + rows)

    def clear_front(r, carry):
        for comp in range(2):
            main[comp, r, pl.ds(0, SUB)] = blank
            main[comp, r, pl.ds(work + SUB, SUB)] = blank
        return carry

    lax.fori_loop(0, tall, clear_front, 0)
    inner = lax.broadcasted_iota(jnp.int32, (width, width), 0)
    outer = lax.broadcasted_iota(jnp.int32, (width, width), 1)
    near = (jnp.abs(inner - outer) <= LOOK).astype(jnp.float32).astype(jnp.bfloat16)
    box[pl.ds(0, width)] = near
    box[pl.ds(width, width)] = near

    def edge_table(g, carry):
        cell = inner - slot * g
        left = (cell >= 0) & (cell < LOOK) & (outer <= cell) & (me > 0)
        if not thin:
            cell = cell - LOOK
        right = (cell >= 0) & (cell < LOOK) & (outer >= width + cell - LOOK) & (me < nd - 1)
        edge = (left | right).astype(jnp.float32).astype(jnp.bfloat16)
        edges[g, pl.ds(0, width)] = edge
        edges[g, pl.ds(width, width)] = edge
        return carry

    lax.fori_loop(0, groups, edge_table, 0)
    for k in range(rows):
        root[k, pl.ds(0, pad)] = jnp.zeros((pad, width), jnp.float32)

    def clear_state(step, carry):
        for d in range(band):
            for comp in range(2):
                vec[step, comp, dates + d] = zero
            for c in range(3):
                acc[step, c, d] = zero
        tot[step] = zero
        return carry

    lax.fori_loop(0, ITERS, clear_state, 0)

    def clear_last(o, carry):
        for c in range(3):
            for d in range(band):
                gam[o, c, pl.ds((pad + dates - band + d) * rows, rows)] = zero
        return carry

    lax.fori_loop(0, band, clear_last, 0)

    pl.semaphore_wait(barrier, nd - 1 + has_up.astype(jnp.int32) + has_down.astype(jnp.int32))
    fetch_own.wait()

    start = FIRST if nd == 2 else parts

    def send(n, carry):
        @pl.when(n < start)
        def _():
            take(0, n)

        @pl.when(n == 0)
        def _():
            for k in range(1, nd):
                give(k, 0).start()
            fetch.wait()
            lax.fori_loop(0, nd, pack_rim, 0)
            start_halos(own, parts)
            for k in range(1, nd):
                give_rim(k).start()

        @pl.when(n > 0)
        def _():
            for k in range(1, nd):
                give(k, n).start()

        return carry

    lax.fori_loop(0, parts, send, 0)

    inner = lax.broadcasted_iota(jnp.int32, (dates, dates), 0)
    outer = lax.broadcasted_iota(jnp.int32, (dates, dates), 1)
    order = (inner == jnp.where(turn, dates - 1 - outer, outer)).astype(jnp.float32).astype(jnp.bfloat16)
    fetch_net.wait()
    mask = jnp.transpose(net_ref[...].astype(jnp.float32), (1, 0)).astype(jnp.bfloat16)
    mask = jnp.dot(order, mask, preferred_element_type=jnp.float32)

    def spread(o, carry):
        column = lax.broadcasted_iota(jnp.int32, (dates, band), 1) == o
        column = jnp.sum(jnp.where(column, mask, 0.0), axis=1, keepdims=True)
        used_at[o, pl.ds(0, pad)] = jnp.zeros((pad, width), jnp.float32)
        used_at[o, pl.ds(pad, dates)] = jnp.broadcast_to(column, (dates, width))
        return carry

    lax.fori_loop(0, band, spread, 0)
    def forward_rim(k):
        give_rim(k).wait_recv()
        start_halos(slab_of(k), parts)

    def forward(k, n):
        give(k, n).wait_recv()
        take(k, n)

    if nd != 2:
        for k in range(1, nd):
            forward_rim(k)
            for n in range(parts):
                forward(k, n)

    lane = lax.broadcasted_iota(jnp.int32, (SUB, width), 1)

    def open_slab(slab):
        def part(comp, carry):
            from_comp = 0 if thin else comp
            last_comp = 1 - comp if thin else comp
            here = [main[from_comp, r, aligned(rims + slab * SUB)] for r in range(tall)]
            last = [main[last_comp, r, pl.ds(work + SUB, SUB)] for r in range(tall)]
            if thin:
                here = [pltpu.roll(cell, comp * (width // 2), 1) for cell in here]
            ends = lane >= width - slot
            earlier = [pltpu.roll(jnp.where(ends, b, a), slot % width, 1) for a, b in zip(here, last)]
            for r in range(tall):
                main[comp, r, pl.ds(work, SUB)] = earlier[r]
                held[comp, r] = here[r]
            return carry

        lax.fori_loop(0, 2, part, 0)

        def keep(r, carry):
            for comp in range(2):
                main[comp, r, pl.ds(work + SUB, SUB)] = held[comp, r]
            return carry

        lax.fori_loop(0, tall, keep, 0)

    def pair_rows(o, base):
        part_re, part_im = [], []
        here, ahead = aligned(base), pl.ds(base - o, SUB)
        for r in range(tall):
            a_re, a_im = main[0, r, ahead], main[1, r, ahead]
            b_re, b_im = main[0, r, here], main[1, r, here]
            part_re.append(a_re * b_re + a_im * b_im)
            part_im.append(a_im * b_re - a_re * b_im)
        return halves(row_sums(part_re) + row_sums(part_im))

    each = 2 * rows * SUB

    def rim_sums():
        base = work + SUB
        rim_maps[pl.ds(0, each // 2)] = square_rows(base)

        def offset(o, carry):
            begin = pl.multiple_of(each // 2 + (o - 1) * each, each // 2)
            rim_maps[pl.ds(begin, each)] = pair_rows(o, base)
            return carry

        lax.fori_loop(1, band + 1, offset, 0)

    def square_rows(base):
        squares = []
        for r in range(tall):
            re, im = main[0, r, aligned(base)], main[1, r, aligned(base)]
            squares.append(re * re + im * im)
        return halves(row_sums(squares))

    def tile_sums(t):
        g = lax.rem(t, groups)
        base = SUB + t * SUB
        to = pad + t * SUB
        here = aligned(to)

        def column_sums(rows_of, begin):
            rim = rim_maps[pl.ds(begin, rows_of.shape[0])]
            table = jnp.concatenate([box[...], edges[g]], axis=0)
            return jnp.dot(jnp.concatenate([rows_of, rim], axis=1), table, preferred_element_type=jnp.float32)

        power = lax.rsqrt(column_sums(square_rows(base), 0) + EPS)
        for k in range(rows):
            root[k, here] = power[k * SUB : (k + 1) * SUB]
        for i in range(0, band, STRIDE):
            begin = each // 2 + i * each
            sums = column_sums(jnp.concatenate([pair_rows(i + s + 1, base) for s in range(STRIDE)], axis=0), begin)
            for s in range(STRIDE):
                o = i + s + 1
                used = used_at[o - 1, pl.ds(jnp.where(turn, to, to - o), SUB)]
                for k in range(rows):
                    weight = root[k, here] * root[k, pl.ds(to - o, SUB)] * used
                    at = pl.ds((to - o) * rows + k, SUB, stride=rows)
                    c_re = sums[s * each + k * SUB : s * each + (k + 1) * SUB] * weight
                    c_im = sums[s * each + (rows + k) * SUB : s * each + (rows + k + 1) * SUB] * weight
                    gam[o - 1, 0, at] = c_re
                    gam[o - 1, 1, at] = c_re + c_im
                    gam[o - 1, 2, at] = c_im - c_re

    def at_date(d):
        return pl.ds(pl.multiple_of((pad + d) * rows, rows), rows)

    def first(j):
        back_re = [acc[0, 0, i] for i in range(band)]
        back_sum = [acc[0, 1, i] for i in range(band)]
        total = tot[0]
        for i in range(SUB):
            d = j * SUB + i
            y_re = back_re[i] + 1.0
            y_im = back_re[i] - back_sum[i]
            ahead_re = ahead_sum = None
            for o in range(1, band + 1):
                c_re = gam[o - 1, 0, at_date(d)]
                c_sum = gam[o - 1, 1, at_date(d)]
                ahead_re = c_re if ahead_re is None else ahead_re + c_re
                ahead_sum = c_sum if ahead_sum is None else ahead_sum + c_sum
                if o == band:
                    back_re.append(c_re)
                    back_sum.append(c_sum)
                else:
                    back_re[i + o] = back_re[i + o] + c_re
                    back_sum[i + o] = back_sum[i + o] + c_sum
            y_re = y_re + ahead_re
            y_im = y_im + (ahead_sum - ahead_re)
            vec[0, 0, d] = y_re
            vec[0, 1, d] = y_im
            total = total + (y_re * y_re + y_im * y_im)
        for i in range(band):
            acc[0, 0, i] = back_re[SUB + i]
            acc[0, 1, i] = back_sum[SUB + i]
        tot[0] = total

    def later(step, j):
        acc_a, acc_b, acc_c = [[acc[step, c, i] for i in range(band)] for c in range(3)]
        base = j * SUB
        v_re = [vec[step - 1, 0, base + i] for i in range(band)]
        v_im = [vec[step - 1, 1, base + i] for i in range(band)]
        v_sum = [a + b for a, b in zip(v_re, v_im)]
        total = tot[step]
        for i in range(SUB):
            d = base + i
            v_re.append(vec[step - 1, 0, d + band])
            v_im.append(vec[step - 1, 1, d + band])
            v_sum.append(v_re[-1] + v_im[-1])
            y_a, y_b, y_c = acc_a[i], -acc_b[i], -acc_c[i]
            for o in range(1, band + 1):
                c_re = gam[o - 1, 0, at_date(d)]
                c_sum = gam[o - 1, 1, at_date(d)]
                c_dif = gam[o - 1, 2, at_date(d)]
                y_a = y_a + c_re * v_sum[i + o]
                y_b = y_b + c_dif * v_re[i + o]
                y_c = y_c + c_sum * v_im[i + o]
                back_a = c_re * v_sum[i]
                back_b = c_sum * v_re[i]
                back_c = c_dif * v_im[i]
                if o == band:
                    acc_a.append(back_a)
                    acc_b.append(back_b)
                    acc_c.append(back_c)
                else:
                    acc_a[i + o] = acc_a[i + o] + back_a
                    acc_b[i + o] = acc_b[i + o] + back_b
                    acc_c[i + o] = acc_c[i + o] + back_c
            y_re = v_re[i] + (y_a - y_c)
            y_im = v_im[i] + (y_a + y_b)
            vec[step, 0, d] = y_re
            vec[step, 1, d] = y_im
            total = total + (y_re * y_re + y_im * y_im)
        for i in range(band):
            acc[step, 0, i] = acc_a[SUB + i]
            acc[step, 1, i] = acc_b[SUB + i]
            acc[step, 2, i] = acc_c[SUB + i]
        tot[step] = total

    def advance(t, carry):
        if nd == 2:

            @pl.when(t < parts - start)
            def _():
                take(0, t + start)

            @pl.when(t == groups - EDGES)
            def _():
                forward_rim(1)

            past = t - groups + AHEAD

            @pl.when((past >= 0) & (lax.rem(past, span) == 0) & (past < groups))
            def _():
                forward(1, lax.div(past, span))

        @pl.when(t < tiles)
        def _():
            slab, g = lax.div(t, groups), lax.rem(t, groups)

            @pl.when(g == 0)
            def _():
                await_halos(slab, parts)
                open_slab(slab)
                rim_sums()

            @pl.when(lax.rem(g, span) == 0)
            def _():
                await_halos(slab, lax.div(g, span))

            tile_sums(t)

        @pl.when((t >= 1) & (t <= tiles))
        def _():
            first(t - 1)

        def level(step, carry):
            later(step, t - 1 - step)
            return carry

        lax.fori_loop(jnp.maximum(1, t - tiles), jnp.minimum(t, ITERS), level, 0)
        return carry

    lax.fori_loop(0, tiles + ITERS, advance, 0)

    def sent(n, carry):
        for k in range(1, nd):
            give(k, n).wait_send()
        for s in range(nd):
            await_sent(s, n)
        return carry

    lax.fori_loop(0, parts, sent, 0)
    for k in range(1, nd):
        give_rim(k).wait_send()
    for s in range(nd):
        await_sent(s, parts)


def scale_kernel(nd, vec, tot, out_ref):
    span = out_ref.shape[1]
    dates = span * STEPS
    scale = None
    for step in range(ITERS):
        mean = tot[step] / dates
        if scale is None:
            scale = lax.rsqrt(mean + EPS)
        else:
            scale = scale * lax.rsqrt(scale * scale * mean + EPS)
    turn = 2 * lax.axis_index("date") >= nd
    begin = pl.program_id(0) * span

    def block(b, carry):
        for j in range(SUB):
            d = b * SUB + j
            at = jnp.where(turn, dates - 1 - begin - d, begin + d)
            for comp in range(2):
                out_ref[comp, d] = vec[ITERS - 1, comp, at] * scale
        return carry

    lax.fori_loop(0, span // SUB, block, 0)


def odd(count):
    return count + 1 - count % 2


def on_device(nd, nr, slc, network):
    _, local, rows, cols = slc.shape
    width = cols // nd
    dates, band = network.shape
    tall = rows + 2 * LOOK
    maps = (2 * band + 1) * rows * SUB
    parts = local // PIECE if local % PIECE == 0 else 1
    whole = pl.BlockSpec(memory_space=pltpu.VMEM)
    away = pl.BlockSpec(memory_space=pltpu.HBM)
    f32, bf16 = jnp.float32, jnp.bfloat16
    sems = pltpu.SemaphoreType.DMA((nd, parts + 1))
    vec, tot = pl.pallas_call(
        functools.partial(main_kernel, nd, nr),
        out_shape=[
            pltpu.VMEM((ITERS, 2, dates + band, rows, width), f32),
            pltpu.VMEM((ITERS, rows, width), f32),
        ],
        in_specs=[away, away],
        out_specs=[whole, whole],
        scratch_shapes=[
            pltpu.VMEM((band, dates), network.dtype),
            pltpu.VMEM((2, local, rows, cols), f32),
            pltpu.VMEM((nd, 2, local, rows, width), f32),
            pltpu.VMEM((2, tall, odd(dates // SUB + 2 * nd + 2) * SUB, width), f32),
            pltpu.VMEM((2, tall, SUB, width), f32),
            pltpu.VMEM((maps, 2 * width), bf16),
            pltpu.VMEM((2 * width, width), bf16),
            pltpu.VMEM((local // SUB, 2 * width, width), bf16),
            pltpu.VMEM((rows, odd((2 * band + dates) // SUB) * SUB, width), f32),
            pltpu.VMEM((band, odd((2 * band + dates) // SUB) * SUB, width), f32),
            pltpu.VMEM((band, 3, odd(2 * band + dates) * rows, width), f32),
            pltpu.VMEM((ITERS, 3, band, rows, width), f32),
            pltpu.SemaphoreType.DMA((3,)),
        ]
        + [sems] * 6,
        compiler_params=pltpu.CompilerParams(
            collective_id=0, has_side_effects=True, vmem_limit_bytes=40 * 1024 * 1024
        ),
        name="link",
    )(pltpu.with_memory_space_constraint(slc, pltpu.HBM), pltpu.with_memory_space_constraint(network.T, pltpu.HBM))
    vec = pltpu.with_memory_space_constraint(vec, pltpu.VMEM)
    tot = pltpu.with_memory_space_constraint(tot, pltpu.VMEM)
    return pl.pallas_call(
        functools.partial(scale_kernel, nd),
        out_shape=jax.ShapeDtypeStruct((2, dates, rows, width), f32),
        in_specs=[whole, whole],
        grid=(STEPS,),
        out_specs=pl.BlockSpec((2, dates // STEPS, rows, width), lambda i: (0, i, 0, 0)),
        compiler_params=pltpu.CompilerParams(vmem_limit_bytes=8 * 1024 * 1024),
        name="scale",
    )(vec, tot)


def solution(mesh):
    return jax.shard_map(
        functools.partial(on_device, mesh.shape["date"], mesh.shape["row"]),
        mesh=mesh,
        in_specs=(P(None, "date", "row", None), P()),
        out_specs=P(None, None, "row", "date"),
        check_vma=False,
    )
```
